128 devices in a mesh: dp: 32 (over x, z, core), head: 4 (over y).
Axes of the slice: x: 4, y: 4, z: 4, core: 2. Of those that a mesh axis runs over, the one named last changes fastest.
Arguments:
- queries: bfloat16 [8192, 64, 128], P('dp', 'head'), may hold values from -32 to 32
- traj_kv: bfloat16 [8192, 8, 2, 128], P('dp', 'head'), may hold values from -6 to 6
- grad_out: bfloat16 [8192, 64, 128], P('dp', 'head'), may hold values from -16 to 16
- doc_kv: bfloat16 [128, 128, 8, 2, 128], P('dp', 'head'), may hold values from -6 to 6
- citations: int32 [32, 16], replicated, may hold values from 0 to 127, as said below
- doc_slot: int32 [128], replicated, may hold values from 0 to 127, as said below
- visible_from: int32 [32, 16], P('dp'), may hold values from 0 to 3
Outputs:
- attended: bfloat16 [8192, 64, 128], P('dp', 'head')
- d_queries: bfloat16 [8192, 64, 128], P('dp', 'head')
- d_traj_kv: bfloat16 [8192, 8, 2, 128], P('dp', 'head')
- d_doc_kv: float32 [128, 128, 8, 2, 128], P('dp', 'head')
The draws below stay inside these ranges and needn't reach their ends.
Inputs may be any that keep to these rules, and one draw needn't show every extreme that they name: `citations`: each row names 16 different documents, no two of them stored on the same owner, where document d is stored on owner doc_slot[d] // 4. A permutation: document d's keys and values are row doc_slot[d] of doc_kv.
All inputs are finite; a program needn't handle non-finite values.
Results may differ from the reference program's by a relative error of at most 0.04.
Values may be sent and summed in bfloat16 or wider, within the bound.
A program may use at most 192 MiB of HBM per device.

```python
import math
import jax
import jax.numpy as jnp
from jax import lax

HEADS = 64
KV_HEADS = 8
HEAD_DIM = 128
TLEN = 256
SEG = 64
DLEN = 128
DOCS_DEV = 4
NTRAJ = 32
TOKENS = 8192
CITES = 16
NDOCS = 128
NSEG = 4
N_DP = 32


def citation_plan(key):
    base = jax.random.fold_in(key, 101)
    key_slot, key_owner, key_hot, key_roll = jax.random.split(base, 4)
    slot_of = jax.random.permutation(key_slot, NDOCS).astype(jnp.int32)
    doc_at = jnp.argsort(slot_of).astype(jnp.int32)
    ranking = jax.random.randint(key_owner, (NTRAJ, N_DP), 0, 1 << 20) * N_DP + jnp.arange(N_DP, dtype=jnp.int32)[None, :]
    owners = jnp.argsort(ranking, axis=1)[:, :CITES].astype(jnp.int32)
    hot = jax.random.randint(key_hot, (N_DP,), 0, DOCS_DEV)
    roll = jax.random.randint(key_roll, (NTRAJ, CITES), 0, 10)
    hot_owner = hot[owners]
    local = jnp.where(roll < 6, hot_owner, (hot_owner + 1 + roll % (DOCS_DEV - 1)) % DOCS_DEV)
    cited = doc_at[owners * DOCS_DEV + local]
    return (slot_of, cited.astype(jnp.int32))


def draw_citations(key, part):
    return citation_plan(key)[1]


def draw_doc_slot(key, part):
    return citation_plan(key)[0]


def draw_queries(key, part):
    shape = (TOKENS, HEADS, HEAD_DIM)
    return jnp.clip(jax.random.normal(jax.random.fold_in(key, 1), shape, jnp.float32), -6.0, 6.0).astype(jnp.bfloat16)


def draw_traj_kv(key, part):
    shape = (TOKENS, KV_HEADS, 2, HEAD_DIM)
    return jnp.clip(jax.random.normal(jax.random.fold_in(key, 1), shape, jnp.float32), -6.0, 6.0).astype(jnp.bfloat16)


def set_ends(drawn, rng, low, largest):
    place = [jax.random.randint(jax.random.fold_in(rng, axis), (), 0, length) for axis, length in enumerate(drawn.shape)]
    longest = drawn.shape.index(max(drawn.shape))
    next_to = place[:longest] + [(place[longest] + 1) % drawn.shape[longest]] + place[longest + 1:]
    return drawn.at[tuple(place)].set(low).at[tuple(next_to)].set(largest)


def steps_of(own_key, dims, cuts, low, top_value):
    level, own = 1.0, jax.random.fold_in(own_key, 6)
    for dim, shards_of in cuts:
        heights = jnp.exp(jax.random.uniform(jax.random.fold_in(own, dim), (shards_of,), jnp.float32, low / len(cuts), top_value / len(cuts)))
        level = level * jnp.repeat(heights, dims[dim] // shards_of).reshape([-1 if axis == dim else 1 for axis in range(len(dims))])
    return level


def normal_values(stream_key, extent, width, most, shards=(), held_as=jnp.bfloat16):
    values = jax.random.normal(stream_key, extent, jnp.float32) * width
    if len(shards) > 0:
        values = steps_of(stream_key, extent, shards, -0.22, 0.18) * values
    return jnp.clip(values, min=-most, max=most).astype(held_as)


def setup_inputs(seed: int = 0) -> dict:
    seeds = jax.random.split(jax.random.key(seed), 8)
    return {
        "queries": draw_queries(jax.random.fold_in(seeds[7], 71), 0),
        "traj_kv": draw_traj_kv(jax.random.fold_in(seeds[7], 71), 0),
        "grad_out": normal_values(seeds[2], (TOKENS, HEADS, HEAD_DIM), 4.0, 16.0, ((0, 32), (1, 4))),
        "doc_kv": normal_values(seeds[3], (NDOCS, DLEN, KV_HEADS, 2, HEAD_DIM), 1.0, 6.0, ((0, 32), (1, 4))),
        "citations": draw_citations(jax.random.fold_in(seeds[7], 71), 0),
        "doc_slot": draw_doc_slot(jax.random.fold_in(seeds[7], 71), 0),
        "visible_from": set_ends(jax.random.randint(seeds[6], (NTRAJ, CITES), 0, NSEG), jax.random.fold_in(seeds[6], 1), 0, NSEG - 1).astype(jnp.int32),
    }


def trajectory(query, own_kv, cotangent, cited_kv, visible):
    group = HEADS // KV_HEADS
    scale = 1.0 / math.sqrt(HEAD_DIM)
    doc_keys_count = CITES * DLEN
    keys = jnp.concatenate([cited_kv[:, :, 0], own_kv[:, :, 0]], 0).astype(jnp.float32)
    value_rows = jnp.concatenate([cited_kv[:, :, 1], own_kv[:, :, 1]], 0).astype(jnp.float32)
    query_float = query.astype(jnp.float32).reshape(TLEN, KV_HEADS, group, HEAD_DIM)
    cotangent_float = cotangent.astype(jnp.float32).reshape(TLEN, KV_HEADS, group, HEAD_DIM)
    position = jnp.arange(TLEN, dtype=jnp.int32)
    segment = position // SEG
    doc_from = jnp.repeat(visible, DLEN)
    mask = jnp.concatenate([segment[:, None] >= doc_from[None, :], position[:, None] >= position[None, :]], 1)
    score = jnp.einsum('tgrd,kgd->grtk', query_float, keys) * scale
    score = jnp.where(mask[None, None], score, -jnp.inf)
    top = lax.optimization_barrier(jnp.max(score, -1, keepdims=True))
    lse = top + jnp.log(lax.optimization_barrier(jnp.sum(jnp.exp(score - top), -1, keepdims=True)))
    prob = jnp.exp(score - lse)
    prob16 = lax.optimization_barrier(prob.astype(jnp.bfloat16)).astype(jnp.float32)
    attended = jnp.einsum('grtk,kgd->tgrd', prob16, value_rows).astype(jnp.bfloat16)
    attention_float = lax.optimization_barrier(attended).astype(jnp.float32)
    output_grad_dot = jnp.einsum('kmjy,kmjy->mjk', cotangent_float, attention_float)
    dprob = jnp.einsum('tgrd,kgd->grtk', cotangent_float, value_rows)
    dscore = lax.optimization_barrier((prob * (dprob - output_grad_dot[..., None]) * scale).astype(jnp.bfloat16)).astype(jnp.float32)
    d_query = jnp.einsum('grtk,kgd->tgrd', dscore, keys).astype(jnp.bfloat16)
    key_part = jnp.einsum('grtk,tgrd->kgd', dscore, query_float)
    value_part = jnp.einsum('grtk,tgrd->kgd', prob16, cotangent_float)
    parts = jnp.stack([key_part, value_part], 2)
    own_grad = parts[doc_keys_count:].astype(jnp.bfloat16)
    doc_grad = parts[:doc_keys_count].astype(jnp.bfloat16)
    return (attended.reshape(TLEN, HEADS, HEAD_DIM), d_query.reshape(TLEN, HEADS, HEAD_DIM), own_grad, doc_grad)

def reference(queries, traj_kv, grad_out, doc_kv, citations, doc_slot, visible_from):
    slots = doc_slot[citations].astype(jnp.int32)
    query_all = queries.reshape(NTRAJ, TLEN, HEADS, HEAD_DIM)
    own_all = traj_kv.reshape(NTRAJ, TLEN, KV_HEADS, 2, HEAD_DIM)
    cot_all = grad_out.reshape(NTRAJ, TLEN, HEADS, HEAD_DIM)

    def one_step(total, item):
        query, own_kv, cotangent, slot_row, visible = item
        cited_kv = doc_kv[slot_row].reshape(CITES * DLEN, KV_HEADS, 2, HEAD_DIM)
        attended, d_query, own_grad, doc_grad = trajectory(query, own_kv, cotangent, cited_kv, visible)
        total = total.at[slot_row].add(doc_grad.astype(jnp.float32).reshape(CITES, DLEN, KV_HEADS, 2, HEAD_DIM))
        return (total, (attended, d_query, own_grad))
    start = jnp.zeros((NDOCS, DLEN, KV_HEADS, 2, HEAD_DIM), jnp.float32)
    total, (attended, d_query, own_grad) = lax.scan(one_step, start, (query_all, own_all, cot_all, slots, visible_from))
    return (attended.reshape(TOKENS, HEADS, HEAD_DIM), d_query.reshape(TOKENS, HEADS, HEAD_DIM), own_grad.reshape(TOKENS, KV_HEADS, 2, HEAD_DIM), total)
```

```python
import math

import jax
import jax.numpy as jnp
from jax import lax
from jax.sharding import PartitionSpec as P

SEG = 64


def body(queries, traj_kv, grad_out, doc_kv, citations, doc_slot, visible_from):
    nhead = lax.axis_size("head")
    me = lax.axis_index("dp")
    tlen, heads_local, hdim = queries.shape
    kv_local = traj_kv.shape[1]
    group = heads_local // kv_local
    docs_dev = doc_kv.shape[0]
    dlen_local = doc_kv.shape[1]
    dlen = dlen_local * nhead
    cites = citations.shape[1]
    ndocs = doc_slot.shape[0]
    width = kv_local * 2 * hdim
    scale = 1.0 / math.sqrt(hdim)
    single_precision = jnp.float32
    bf16 = jnp.bfloat16
    match = citations[:, :, None] == jnp.arange(ndocs, dtype=jnp.int32)[None, None, :]
    slots = jnp.sum(jnp.where(match, doc_slot[None, None, :], 0), -1)
    owners = slots // docs_dev
    local = slots % docs_dev
    mine = owners == me
    sends = jnp.any(mine, 1)
    send_local = jnp.sum(jnp.where(mine, local, 0), 1)
    stored = lax.all_to_all(
        doc_kv.reshape(docs_dev, dlen_local, nhead, width), "head", split_axis=2, concat_axis=1, tiled=True
    ).reshape(docs_dev, dlen, width)
    arrived = lax.all_to_all(stored[send_local], "dp", split_axis=0, concat_axis=0, tiled=True)
    own_owners = lax.dynamic_index_in_dim(owners, me, 0, keepdims=False)
    own_slots = lax.dynamic_index_in_dim(slots, me, 0, keepdims=False)
    cited = arrived[own_owners].reshape(cites * dlen, kv_local, 2, hdim)
    doc_keys = cited[:, :, 0]
    doc_vals = cited[:, :, 1]
    self_keys = traj_kv[:, :, 0]
    self_vals = traj_kv[:, :, 1]
    doc_from = jnp.repeat(visible_from[0], dlen)
    key_pos = jnp.arange(tlen, dtype=jnp.int32)

    def segment_step(index, carry):
        out_all, dq_all, grad_dk, grad_dv, grad_sk, grad_sv = carry
        low = index * SEG
        query_block = lax.dynamic_slice_in_dim(queries, low, SEG, 0).reshape(
            SEG, kv_local, group, hdim
        )
        cotangent_block_rows = lax.dynamic_slice_in_dim(grad_out, low, SEG, 0).reshape(
            SEG, kv_local, group, hdim
        )
        rows = low + jnp.arange(SEG, dtype=jnp.int32)
        doc_mask = ((rows // SEG)[:, None] >= doc_from[None, :])[None, None]
        causal = (rows[:, None] >= key_pos[None, :])[None, None]
        score_doc = (
            jnp.einsum(
                "tgrd,kgd->grtk", query_block, doc_keys, preferred_element_type=single_precision
            )
            * scale
        )
        score_self = (
            jnp.einsum(
                "tgrd,kgd->grtk", query_block, self_keys, preferred_element_type=single_precision
            )
            * scale
        )
        score_doc = jnp.where(doc_mask, score_doc, -jnp.inf)
        score_self = jnp.where(causal, score_self, -jnp.inf)
        top = jnp.maximum(jnp.max(score_doc, -1), jnp.max(score_self, -1))[..., None]
        total = jnp.sum(jnp.exp(score_doc - top), -1) + jnp.sum(jnp.exp(score_self - top), -1)
        lse = top + jnp.log(total)[..., None]
        prob_doc = jnp.exp(score_doc - lse)
        prob_self = jnp.exp(score_self - lse)
        prob_doc16 = prob_doc.astype(bf16)
        prob_self16 = prob_self.astype(bf16)
        attention_output = (
            jnp.einsum(
                "grtk,kgd->tgrd", prob_doc16, doc_vals, preferred_element_type=single_precision
            )
            + jnp.einsum(
                "grtk,kgd->tgrd", prob_self16, self_vals, preferred_element_type=single_precision
            )
        ).astype(bf16)
        output_grad_dot = jnp.einsum(
            "kmjy,kmjy->mjk",
            cotangent_block_rows,
            attention_output,
            preferred_element_type=single_precision,
        )[..., None]
        dprob_doc = jnp.einsum(
            "tgrd,kgd->grtk",
            cotangent_block_rows,
            doc_vals,
            preferred_element_type=single_precision,
        )
        dprob_self = jnp.einsum(
            "tgrd,kgd->grtk",
            cotangent_block_rows,
            self_vals,
            preferred_element_type=single_precision,
        )
        dscore_doc = (prob_doc * (dprob_doc - output_grad_dot) * scale).astype(bf16)
        dscore_self = (prob_self * (dprob_self - output_grad_dot) * scale).astype(bf16)
        d_query = (
            jnp.einsum(
                "grtk,kgd->tgrd", dscore_doc, doc_keys, preferred_element_type=single_precision
            )
            + jnp.einsum(
                "grtk,kgd->tgrd", dscore_self, self_keys, preferred_element_type=single_precision
            )
        ).astype(bf16)
        grad_dk = grad_dk + jnp.einsum(
            "grtk,tgrd->kgd", dscore_doc, query_block, preferred_element_type=single_precision
        )
        grad_dv = grad_dv + jnp.einsum(
            "grtk,tgrd->kgd",
            prob_doc16,
            cotangent_block_rows,
            preferred_element_type=single_precision,
        )
        grad_sk = grad_sk + jnp.einsum(
            "grtk,tgrd->kgd", dscore_self, query_block, preferred_element_type=single_precision
        )
        grad_sv = grad_sv + jnp.einsum(
            "grtk,tgrd->kgd",
            prob_self16,
            cotangent_block_rows,
            preferred_element_type=single_precision,
        )
        out_all = lax.dynamic_update_slice_in_dim(
            out_all, attention_output.reshape(SEG, heads_local, hdim), low, 0
        )
        dq_all = lax.dynamic_update_slice_in_dim(
            dq_all, d_query.reshape(SEG, heads_local, hdim), low, 0
        )
        return (out_all, dq_all, grad_dk, grad_dv, grad_sk, grad_sv)

    start = (
        jnp.zeros((tlen, heads_local, hdim), bf16),
        jnp.zeros((tlen, heads_local, hdim), bf16),
        jnp.zeros((cites * dlen, kv_local, hdim), single_precision),
        jnp.zeros((cites * dlen, kv_local, hdim), single_precision),
        jnp.zeros((tlen, kv_local, hdim), single_precision),
        jnp.zeros((tlen, kv_local, hdim), single_precision),
    )
    attended, d_queries, grad_dk, grad_dv, grad_sk, grad_sv = lax.fori_loop(
        0, tlen // SEG, segment_step, start
    )
    d_traj = jnp.stack([grad_sk, grad_sv], 2).astype(bf16)
    partial_value = jnp.stack([grad_dk, grad_dv], 2).astype(bf16).reshape(cites, dlen, width)
    to_owner = own_owners[None, :] == jnp.arange(ndocs // docs_dev, dtype=jnp.int32)[:, None]
    cite_of = jnp.sum(jnp.where(to_owner, jnp.arange(cites, dtype=jnp.int32)[None, :], 0), 1)
    returned = lax.all_to_all(partial_value[cite_of], "dp", split_axis=0, concat_axis=0, tiled=True)
    pick = (sends[None, :] & (send_local[None, :] == jnp.arange(docs_dev, dtype=jnp.int32)[:, None])).astype(bf16)
    reduced = jnp.einsum("st,tkw->skw", pick, returned, preferred_element_type=single_precision)
    summed = lax.all_to_all(
        reduced.astype(bf16).reshape(docs_dev, dlen, 1, width), "head", split_axis=1, concat_axis=2, tiled=True
    ).astype(single_precision)
    d_doc = summed.reshape(docs_dev, dlen_local, nhead * kv_local, 2, hdim)
    return (attended, d_queries, d_traj, d_doc)


def solution(mesh):
    in_specs = (
        P("dp", "head", None),
        P("dp", "head", None, None),
        P("dp", "head", None),
        P("dp", "head", None, None, None),
        P(),
        P(),
        P("dp", None),
    )
    out_specs = (
        P("dp", "head", None),
        P("dp", "head", None),
        P("dp", "head", None, None),
        P("dp", "head", None, None, None),
    )
    return jax.shard_map(body, mesh=mesh, in_specs=in_specs, out_specs=out_specs, check_vma=False)
```

```python
import functools, math
import jax, jax.numpy as jnp
from jax import lax
from jax.experimental import pallas as pl
from jax.experimental.pallas import tpu as pltpu
from jax.sharding import PartitionSpec as P

SEG=64
BIG=3.0e38
NT=(((1,),(1,)),((),()))
NN=(((1,),(0,)),((),()))
f32=jnp.float32
bf16=jnp.bfloat16

def attn_body(own_ref, vis_ref, cite_ref, q_ref, g_ref, kv_ref, doc_ref, *rest):
    o_ref, dq_ref, dkv_ref, dx_ref, qs, gs, gn, ks, vs, kt, vt, sc, pp, dd, dk, dv = rest[-16:]
    tlen, hdim = q_ref.shape[0], q_ref.shape[2]
    group = q_ref.shape[1]
    cites = own_ref.shape[0]
    dlen = doc_ref.shape[1]
    ndoc = cites*dlen
    nown = doc_ref.shape[0]
    rows = SEG*group
    nseg = tlen//SEG
    scale = 1.0/math.sqrt(hdim)
    c1 = scale*math.log2(math.e)
    nch = ndoc//(2*dlen)
    qs[...] = q_ref[...].astype(f32).reshape(tlen*group, hdim).astype(bf16)
    gs[...] = g_ref[...].astype(f32).reshape(tlen*group, hdim)
    @pl.loop(0, cites)
    def _(c):
        blk = doc_ref[own_ref[c]]
        r = pl.ds(pl.multiple_of(c*dlen, dlen), dlen)
        ks[r, :] = blk[:, :hdim]
        vs[r, :] = blk[:, hdim:]
        kt[:, r] = blk[:, :hdim].T
        vt[:, r] = blk[:, hdim:].T
    own = kv_ref[...]
    ks[ndoc:, :] = own[:, :hdim]
    vs[ndoc:, :] = own[:, hdim:]
    kt[:, ndoc:] = own[:, :hdim].T
    vt[:, ndoc:] = own[:, hdim:].T

    @pl.loop(0, nseg)
    def _(s):
        rs = pl.ds(pl.multiple_of(s*rows, rows), rows)
        q = qs[rs, :]
        m = jnp.full((8, rows), -BIG, f32)
        for c in range(nch + 1):
            r = slice(c*2*dlen, (c+1)*2*dlen)
            st = lax.dot_general(ks[r, :], q, NT, preferred_element_type=f32)
            if c == nch:
                key = lax.broadcasted_iota(jnp.int32, (tlen, rows), 0)
                tok = s*SEG + lax.broadcasted_iota(jnp.int32, (tlen, rows), 1)//group
                st = jnp.where(key <= tok, st, -BIG)
                m = jnp.maximum(m, jnp.max(st.reshape(tlen//8, 8, rows), axis=0))
            else:
                for h in range(2):
                    t = jnp.max(st[h*dlen:(h+1)*dlen].reshape(dlen//8, 8, rows), axis=0)
                    m = jnp.maximum(m, jnp.where(s >= vis_ref[2*c+h], t, -BIG))
            sc[r, :] = st
        m = jnp.max(m, axis=0, keepdims=True)
        l = jnp.zeros((8, rows), f32)
        for c in range(nch + 1):
            for h in range(2):
                r = slice((2*c+h)*dlen, (2*c+h+1)*dlen)
                mm = m if c == nch else jnp.where(s >= vis_ref[2*c+h], m, BIG)
                p = jnp.exp2((sc[r, :] - mm)*c1)
                l = l + jnp.sum(p.reshape(dlen//8, 8, rows), axis=0)
                pp[r, rs] = p.astype(bf16)
        ot = lax.dot_general(vt[...], pp[:, rs], NN, preferred_element_type=f32)
        inv = 1.0/jnp.sum(l, axis=0, keepdims=True)
        o16 = (ot*inv).astype(bf16)
        ot = o16.astype(f32)
        o_ref[pl.ds(pl.multiple_of(s*SEG, SEG), SEG)] = ot.T.reshape(SEG, group, hdim).astype(bf16)
        gt = gs[rs, :].T
        delta = jnp.sum(ot*gt, axis=0, keepdims=True)*inv
        gt = gt*inv
        gn[rs, :] = gt.T.astype(bf16)
        gt = gt.astype(bf16)
        for c in range(nch + 1):
            r = slice(c*2*dlen, (c+1)*2*dlen)
            dp = lax.dot_general(vs[r, :], gt, NN, preferred_element_type=f32)
            dd[r, rs] = pp[r, rs]*(dp - delta).astype(bf16)
        dqt = lax.dot_general(kt[...], dd[:, rs], NN, preferred_element_type=f32)*scale
        dq_ref[pl.ds(pl.multiple_of(s*SEG, SEG), SEG)] = dqt.T.reshape(SEG, group, hdim).astype(bf16)
    @pl.loop(0, (nch + 1)//3)
    def _(c):
        r = pl.ds(pl.multiple_of(c*6*dlen, 6*dlen), 6*dlen)
        dk[r, :] = lax.dot_general(dd[r, :], qs[...], NN, preferred_element_type=f32)
        dv[r, :] = lax.dot_general(pp[r, :], gn[...], NN, preferred_element_type=f32)
    dkv_ref[:, :hdim] = (dk[ndoc:, :]*scale).astype(bf16)
    dkv_ref[:, hdim:] = dv[ndoc:, :].astype(bf16)
    @pl.loop(0, nown)
    def _(o):
        r = pl.ds(pl.multiple_of(cite_ref[o]*dlen, dlen), dlen)
        dx_ref[o, :, :hdim] = (dk[r, :]*scale).astype(bf16)
        dx_ref[o, :, hdim:] = dv[r, :].astype(bf16)

def attn(part, own, vis, cite, q4, g4, kv, docs, before=()):
    tlen, nkv, group, hdim = q4.shape
    nown, dlen, _ = docs.shape
    cites = own.shape[0]
    keys = cites*dlen + tlen
    rows = SEG*group
    sq = pl.Squeezed()
    qspec = pl.BlockSpec((tlen, sq, group, hdim), lambda g, *_: (0, part, 0, 0))
    kvspec = pl.BlockSpec((tlen, 2*hdim), lambda g, *_: (0, part))
    dspec = pl.BlockSpec((nown, dlen, 2*hdim), lambda g, *_: (0, 0, 0))
    macs = tlen*group*keys*hdim
    return pl.pallas_call(
        attn_body,
        out_shape=(jax.ShapeDtypeStruct(q4.shape, bf16), jax.ShapeDtypeStruct(q4.shape, bf16),
                   jax.ShapeDtypeStruct(kv.shape, bf16), jax.ShapeDtypeStruct(docs.shape, bf16)),
        grid_spec=pltpu.PrefetchScalarGridSpec(
            num_scalar_prefetch=3, grid=(1,),
            in_specs=[qspec, qspec, kvspec, dspec] + [pl.BlockSpec(memory_space=pl.ANY)]*len(before),
            out_specs=(qspec, qspec, kvspec, dspec),
            scratch_shapes=[
                pltpu.VMEM((tlen*group, hdim), bf16), pltpu.VMEM((tlen*group, hdim), f32), pltpu.VMEM((tlen*group, hdim), bf16),
                pltpu.VMEM((keys, hdim), bf16), pltpu.VMEM((keys, hdim), bf16),
                pltpu.VMEM((hdim, keys), bf16), pltpu.VMEM((hdim, keys), bf16),
                pltpu.VMEM((keys, rows), f32), pltpu.VMEM((keys, tlen*group), bf16), pltpu.VMEM((keys, tlen*group), bf16),
                pltpu.VMEM((keys, hdim), f32), pltpu.VMEM((keys, hdim), f32),
            ]),
        input_output_aliases={7+i: i for i in range(len(before))},
        compiler_params=pltpu.CompilerParams(vmem_limit_bytes=56 << 20),
        cost_estimate=pl.CostEstimate(flops=12*macs, bytes_accessed=8 << 20, transcendentals=tlen*group*keys),
        name="attn",
    )(own, vis, cite, q4, g4, kv, docs, *before)


def body(queries, traj_kv, grad_out, doc_kv, citations, doc_slot, visible_from):
    nhead = lax.axis_size("head")
    me = lax.axis_index("dp")
    tlen, heads_local, hdim = queries.shape
    kv_local = traj_kv.shape[1]
    group = heads_local // kv_local
    docs_dev, dlen_local = doc_kv.shape[:2]
    dlen = dlen_local * nhead
    cites = citations.shape[1]
    ndocs = doc_slot.shape[0]
    width = kv_local * 2 * hdim
    match = citations[:, :, None] == jnp.arange(ndocs, dtype=jnp.int32)[None, None, :]
    slots = jnp.sum(jnp.where(match, doc_slot[None, None, :], 0), -1)
    owners = slots // docs_dev
    mine = owners == me
    sends = jnp.any(mine, 1)
    send_local = jnp.sum(jnp.where(mine, slots % docs_dev, 0), 1)
    own_owners = lax.dynamic_index_in_dim(owners, me, 0, keepdims=False)
    to_owner = own_owners[None, :] == jnp.arange(ndocs // docs_dev, dtype=jnp.int32)[:, None]
    cite_of = jnp.sum(jnp.where(to_owner, jnp.arange(cites, dtype=jnp.int32)[None, :], 0), 1)
    stored = lax.all_to_all(
        doc_kv.reshape(docs_dev, dlen_local, nhead, width), "head", split_axis=2, concat_axis=1, tiled=True
    ).reshape(docs_dev, dlen, width)
    split = (tlen, kv_local, group, hdim)
    q4, g4, kv = queries.reshape(split), grad_out.reshape(split), traj_kv.reshape(tlen, width)
    vis = visible_from[0]
    outgoing = [stored[:, :, g * 2 * hdim : (g + 1) * 2 * hdim][send_local] for g in range(kv_local)]
    pick = (sends[None, :] & (send_local[None, :] == jnp.arange(docs_dev, dtype=jnp.int32)[:, None])).astype(bf16)
    before, partials = (), []
    arrived = lax.all_to_all(outgoing[0], "dp", split_axis=0, concat_axis=0, tiled=True)
    for g in range(kv_local):
        if g + 1 < kv_local:
            arrived, held = lax.optimization_barrier((arrived, outgoing[g + 1]))
            later = lax.all_to_all(held, "dp", split_axis=0, concat_axis=0, tiled=True)
        *before, partial = attn(g, own_owners, vis, cite_of, q4, g4, kv, arrived, before)
        partials.append(partial)
        if g + 1 < kv_local:
            arrived = later
    reduced = []
    for g in range(kv_local):
        if g:
            partials[g], returned = lax.optimization_barrier((partials[g], returned))
        returned = lax.all_to_all(partials[g], "dp", split_axis=0, concat_axis=0, tiled=True)
        reduced.append(jnp.einsum("st,tkw->skw", pick, returned, preferred_element_type=f32).astype(bf16))
    attended, d_queries, d_traj = before
    summed = lax.all_to_all(
        jnp.concatenate(reduced, -1).reshape(docs_dev, dlen, 1, width), "head", split_axis=1, concat_axis=2, tiled=True
    ).astype(f32)
    return (attended.reshape(queries.shape), d_queries.reshape(queries.shape), d_traj.reshape(traj_kv.shape),
            summed.reshape(docs_dev, dlen_local, nhead * kv_local, 2, hdim))


def solution(mesh):
    in_specs = (
        P("dp", "head", None),
        P("dp", "head", None, None),
        P("dp", "head", None),
        P("dp", "head", None, None, None),
        P(),
        P(),
        P("dp", None),
    )
    out_specs = (
        P("dp", "head", None),
        P("dp", "head", None),
        P("dp", "head", None, None),
        P("dp", "head", None, None, None),
    )
    return jax.shard_map(body, mesh=mesh, in_specs=in_specs, out_specs=out_specs, check_vma=False)
```

```python
import functools
import math

import jax
import jax.numpy as jnp
from jax import lax
from jax.experimental import pallas as pl
from jax.experimental.pallas import tpu as pltpu
from jax.sharding import PartitionSpec as P

SEG = 64
BIG = 3.0e38
NT = (((1,), (1,)), ((), ()))
NN = (((1,), (0,)), ((), ()))
NX, NZ, NC, NY = 4, 4, 2, 4
FAR = (2, 1, 3)
f32 = jnp.float32
bf16 = jnp.bfloat16


def kernel(tab, q_ref, g_ref, kv_ref, own_ref, o_ref, dq_ref, dkv_ref, dd_ref, *scratch):
    (qs, gs, gn, ks, vs, kt, vt, sc, pp, ds, dk, dv) = scratch[:12]
    bufs = scratch[12:]
    st, rowk, rowv, sendk, sendv, recvk, recvv, backk, backv, sumk, sumv, tot, home = (
        bufs[2 * i : 2 * i + 2] for i in range(13)
    )
    sems = bufs[26:]
    me, y = lax.axis_index("dp"), lax.axis_index("head")
    x, z, c = me // (NZ * NC), (me // NC) % NZ, me % NC
    tlen, nkv, group, hdim = q_ref.shape
    dlen = st[0].shape[2]
    cites = tab.shape[1] // 2
    ndoc = cites * dlen
    rows = SEG * group
    nseg = tlen // SEG
    nch = ndoc // (2 * dlen)
    scale = 1.0 / math.sqrt(hdim)
    c1 = scale * math.log2(math.e)
    part = dlen // NY
    KIDX, VIDX, VIS, KCITE, VCITE, KRED, VRED = range(7)

    def at(dx, dz, dc, dy):
        dp = (((x + dx) % NX) * NZ + (z + dz) % NZ) * NC + (c + dc) % NC
        return (dp, (y + dy) % NY)

    def copy(stage, g, i, src, dst, to):
        return pltpu.make_async_remote_copy(
            src_ref=src, dst_ref=dst, send_sem=sems[2 * stage].at[g, i], recv_sem=sems[2 * stage + 1].at[g, i],
            device_id=at(*to), device_id_type=pl.DeviceIdType.MESH)

    def heads_out(g):
        return [copy(0, g, i, own_ref.at[(y + dy) % NY, g], st[g].at[:, :, pl.ds(pl.multiple_of(y * part, part), part), :],
                     (0, 0, 0, dy)) for i, dy in enumerate(FAR)]

    def lines_out(g):
        k = [copy(1, g, i, st[g].at[0], rowk[g].at[pl.ds(x * 4, 4)], (d, 0, 0, 0)) for i, d in enumerate(FAR)]
        v = [copy(1, g, 3 + i, st[g].at[1], rowv[g].at[pl.ds(z * 4, 4)], (0, d, 0, 0)) for i, d in enumerate(FAR)]
        return [a for ab in zip(k, v) for a in ab]

    def cross(stage, g, srck, dstk, srcv, dstv):
        hops = [(d, dc) for d in FAR for dc in range(NC)] + [(0, 1)]
        res = []
        for i, (d, dc) in enumerate(hops):
            other = (c + dc) % NC
            jk = ((z + d) % NZ) * NC + other
            jv = ((x + d) % NX) * NC + other
            res.append(copy(stage, g, i, srck[g].at[pl.ds(jk * 4, 4)], dstk[g].at[pl.ds((z * NC + c) * 4, 4)], (0, d, dc, 0)))
            res.append(copy(stage, g, 7 + i, srcv[g].at[pl.ds(jv * 4, 4)], dstv[g].at[pl.ds((x * NC + c) * 4, 4)], (d, 0, dc, 0)))
        return res

    def docs_out(g):
        return cross(2, g, sendk, recvk, sendv, recvv)

    def grads_out(g):
        return cross(3, g, sendk, backk, sendv, backv)

    def sums_out(g):
        k = [copy(4, g, i, rowk[g].at[pl.ds((x + d) % NX * 4, 4)], sumk[g].at[pl.ds(x * 4, 4)], (d, 0, 0, 0))
             for i, d in enumerate(FAR)]
        v = [copy(4, g, 3 + i, rowv[g].at[pl.ds((z + d) % NZ * 4, 4)], sumv[g].at[pl.ds(z * 4, 4)], (0, d, 0, 0))
             for i, d in enumerate(FAR)]
        return [a for ab in zip(k, v) for a in ab]

    def heads_home(g):
        return [copy(5, g, i, tot[g].at[:, :, pl.ds(pl.multiple_of((y + dy) % NY * part, part), part), :], home[g].at[y],
                     (0, 0, 0, dy)) for i, dy in enumerate(FAR)]

    def start(copies):
        for a in copies:
            a.start()

    def wait(copies):
        for a in copies:
            a.wait()

    def send_lines(g):
        wait(heads_out(g))
        start(lines_out(g))
        rowk[g][pl.ds(x * 4, 4)] = st[g][0]
        rowv[g][pl.ds(z * 4, 4)] = st[g][1]

    def send_docs(g):
        wait(lines_out(g))

        @pl.loop(0, 32)
        def _(j):
            sendk[g][j] = rowk[g][j % 4 * 4 + jnp.maximum(tab[KRED, j], 0)]
            sendv[g][j] = rowv[g][j % 4 * 4 + jnp.maximum(tab[VRED, j], 0)]

        keep(g, recvk, recvv)
        start(docs_out(g))

    def keep(g, dstk, dstv):
        jk, jv = (z * NC + c) * 4, (x * NC + c) * 4
        dstk[g][pl.ds(jk, 4)] = sendk[g][pl.ds(jk, 4)]
        dstv[g][pl.ds(jv, 4)] = sendv[g][pl.ds(jv, 4)]

    def gather(g):
        wait(docs_out(g))

        @pl.loop(0, cites)
        def _(i):
            r = pl.ds(pl.multiple_of(i * dlen, dlen), dlen)
            k = recvk[g][tab[KIDX, i]]
            v = recvv[g][tab[VIDX, i]]
            ks[r, :] = k
            vs[r, :] = v
            kt[:, r] = k.T
            vt[:, r] = v.T

    def send_grads(g):
        @pl.loop(0, 32)
        def _(j):
            sendk[g][j] = (dk[tab[KCITE, j]] * scale).astype(bf16)
            sendv[g][j] = dv[tab[VCITE, j]].astype(bf16)

        keep(g, backk, backv)
        start(grads_out(g))

    def send_sums(g):
        wait(grads_out(g))
        for back, row, red in ((backk, rowk, KRED), (backv, rowv, VRED)):
            @pl.loop(0, 4)
            def _(o):
                for h in range(2):
                    r = slice(h * dlen // 2, (h + 1) * dlen // 2)
                    acc = [jnp.zeros((dlen // 2, hdim), f32)] * 4
                    for t in range(8):
                        blk = back[g][t * 4 + o, r]
                        w = tab[red, t * 4 + o]
                        for d in range(4):
                            acc[d] = acc[d] + jnp.where(w == d, blk, jnp.zeros_like(blk)).astype(f32)
                    for d in range(4):
                        row[g][o * 4 + d, r] = acc[d].astype(bf16)

        start(sums_out(g))
        sumk[g][pl.ds(x * 4, 4)] = rowk[g][pl.ds(x * 4, 4)]
        sumv[g][pl.ds(z * 4, 4)] = rowv[g][pl.ds(z * 4, 4)]

    def send_home(g):
        wait(sums_out(g))
        for h, s in enumerate((sumk, sumv)):
            for d in range(4):
                tot[g][h, d] = (s[g][d].astype(f32) + s[g][4 + d].astype(f32)
                                + s[g][8 + d].astype(f32) + s[g][12 + d].astype(f32)).astype(bf16)
        start(heads_home(g))
        home[g][y] = tot[g][:, :, pl.ds(pl.multiple_of(y * part, part), part), :]

    barrier = pltpu.get_barrier_semaphore()
    near = [(d, 0, dc, 0) for d in range(NX) for dc in range(NC) if d or dc]
    near += [(0, d, dc, 0) for d in FAR for dc in range(NC)] + [(0, 0, 0, d) for d in FAR]
    for to in near:
        pl.semaphore_signal(barrier, inc=1, device_id=at(*to), device_id_type=pl.DeviceIdType.MESH)
    pl.semaphore_wait(barrier, len(near))

    for g in range(2):
        start(heads_out(g))
        st[g][:, :, pl.ds(pl.multiple_of(y * part, part), part), :] = own_ref[y, g]
    send_lines(0)
    send_docs(0)

    @pl.loop(0, nkv)
    def _(g):
        half = pl.ds(pl.multiple_of(g * 2 * hdim, 2 * hdim), 2 * hdim)
        qs[...] = q_ref[:, g].astype(f32).reshape(tlen * group, hdim).astype(bf16)
        gs[...] = g_ref[:, g].astype(f32).reshape(tlen * group, hdim)
        own = kv_ref[:, half]
        ks[ndoc:, :] = own[:, :hdim]
        vs[ndoc:, :] = own[:, hdim:]
        kt[:, ndoc:] = own[:, :hdim].T
        vt[:, ndoc:] = own[:, hdim:].T

        @pl.when(g == 0)
        def _():
            gather(0)
            send_lines(1)

        @pl.when(g == 1)
        def _():
            gather(1)

        @pl.loop(0, nseg)
        def _(s):
            @pl.when((g == 0) & (s == 2))
            def _():
                send_docs(1)

            @pl.when((g == 1) & (s == 3))
            def _():
                send_sums(0)

            rs = pl.ds(pl.multiple_of(s * rows, rows), rows)
            q = qs[rs, :]
            m = jnp.full((8, rows), -BIG, f32)
            for i in range(nch + 1):
                r = slice(i * 2 * dlen, (i + 1) * 2 * dlen)
                score = lax.dot_general(ks[r, :], q, NT, preferred_element_type=f32)
                if i == nch:
                    key = lax.broadcasted_iota(jnp.int32, (tlen, rows), 0)
                    tok = s * SEG + lax.broadcasted_iota(jnp.int32, (tlen, rows), 1) // group
                    score = jnp.where(key <= tok, score, -BIG)
                    m = jnp.maximum(m, jnp.max(score.reshape(tlen // 8, 8, rows), axis=0))
                else:
                    for h in range(2):
                        t = jnp.max(score[h * dlen : (h + 1) * dlen].reshape(dlen // 8, 8, rows), axis=0)
                        m = jnp.maximum(m, jnp.where(s >= tab[VIS, 2 * i + h], t, -BIG))
                sc[r, :] = score
            m = jnp.max(m, axis=0, keepdims=True)
            total = jnp.zeros((8, rows), f32)
            for i in range(2 * nch + 2):
                r = slice(i * dlen, (i + 1) * dlen)
                mm = m if i >= 2 * nch else jnp.where(s >= tab[VIS, i], m, BIG)
                p = jnp.exp2((sc[r, :] - mm) * c1)
                total = total + jnp.sum(p.reshape(dlen // 8, 8, rows), axis=0)
                pp[r, rs] = p.astype(bf16)
            ot = lax.dot_general(vt[...], pp[:, rs], NN, preferred_element_type=f32)
            inv = 1.0 / jnp.sum(total, axis=0, keepdims=True)
            ot = (ot * inv).astype(bf16).astype(f32)
            block = pl.ds(pl.multiple_of(s * SEG, SEG), SEG)
            o_ref[block, g] = ot.T.reshape(SEG, group, hdim).astype(bf16)
            gt = gs[rs, :].T
            delta = jnp.sum(ot * gt, axis=0, keepdims=True) * inv
            gt = gt * inv
            gn[rs, :] = gt.T.astype(bf16)
            gt = gt.astype(bf16)
            for i in range(nch + 1):
                r = slice(i * 2 * dlen, (i + 1) * 2 * dlen)
                dp = lax.dot_general(vs[r, :], gt, NN, preferred_element_type=f32)
                ds[r, rs] = pp[r, rs] * (dp - delta).astype(bf16)
            dqt = lax.dot_general(kt[...], ds[:, rs], NN, preferred_element_type=f32) * scale
            dq_ref[block, g] = dqt.T.reshape(SEG, group, hdim).astype(bf16)

        @pl.loop(0, (nch + 1) // 3)
        def _(i):
            r = pl.ds(pl.multiple_of(i * 6 * dlen, 6 * dlen), 6 * dlen)
            b = pl.ds(i * 6, 6)
            dk[b] = lax.dot_general(ds[r, :], qs[...], NN, preferred_element_type=f32).reshape(6, dlen, hdim)
            dv[b] = lax.dot_general(pp[r, :], gn[...], NN, preferred_element_type=f32).reshape(6, dlen, hdim)

        @pl.when(g == 0)
        def _():
            send_grads(0)

        @pl.when(g == 1)
        def _():
            send_grads(1)

        own_k = dk[cites:].reshape(tlen, hdim) * scale
        dkv_ref[:, half] = jnp.concatenate([own_k, dv[cites:].reshape(tlen, hdim)], axis=1).astype(bf16)

    send_home(0)
    send_sums(1)
    wait(heads_home(0))
    dd_ref[:, 0] = home[0][...].astype(f32)
    send_home(1)
    wait(heads_home(1))
    dd_ref[:, 1] = home[1][...].astype(f32)


def attention(tab, q4, g4, kv, own):
    tlen, nkv, group, hdim = q4.shape
    dlen = own.shape[0] * own.shape[4]
    cites = tab.shape[1] // 2
    keys = cites * dlen + tlen
    rows, all_rows = SEG * group, tlen * group
    macs = all_rows * keys * hdim * nkv

    def vmem(shape, dtype=bf16):
        return pltpu.VMEM(shape, dtype)

    blocks = lambda n: [vmem((n, dlen, hdim))] * 2
    scratch = [
        vmem((all_rows, hdim)), vmem((all_rows, hdim), f32), vmem((all_rows, hdim)),
        vmem((keys, hdim)), vmem((keys, hdim)), vmem((hdim, keys)), vmem((hdim, keys)),
        vmem((keys, rows), f32), vmem((keys, all_rows)), vmem((keys, all_rows)),
        vmem((keys // dlen, dlen, hdim), f32), vmem((keys // dlen, dlen, hdim), f32),
    ]
    scratch += [vmem((2, 4, dlen, hdim))] * 2
    scratch += blocks(16) + blocks(16)
    scratch += blocks(32) * 6
    scratch += blocks(16) + blocks(16)
    scratch += [vmem((2, 4, dlen, hdim))] * 2
    scratch += [vmem((NY, 2, 4, dlen // NY, hdim))] * 2
    for n in (3, 6, 14, 14, 6, 3):
        scratch += [pltpu.SemaphoreType.DMA((2, n))] * 2
    whole = pl.BlockSpec(memory_space=pltpu.VMEM)
    return pl.pallas_call(
        kernel,
        out_shape=(jax.ShapeDtypeStruct(q4.shape, bf16), jax.ShapeDtypeStruct(q4.shape, bf16),
                   jax.ShapeDtypeStruct(kv.shape, bf16), jax.ShapeDtypeStruct(own.shape, f32)),
        in_specs=[pl.BlockSpec(memory_space=pltpu.SMEM)] + [whole] * 4,
        out_specs=(whole,) * 4,
        scratch_shapes=scratch,
        compiler_params=pltpu.CompilerParams(
            collective_id=0, has_side_effects=True, vmem_limit_bytes=67043328),
        cost_estimate=pl.CostEstimate(flops=12 * macs, bytes_accessed=8 << 20, transcendentals=macs // hdim),
        name="attention",
    )(tab, q4, g4, kv, own)


def body(queries, traj_kv, grad_out, doc_kv, citations, doc_slot, visible_from):
    me = lax.axis_index("dp")
    x, z, c = me // (NZ * NC), (me // NC) % NZ, me % NC
    tlen, heads_local, hdim = queries.shape
    kv_local = traj_kv.shape[1]
    group = heads_local // kv_local
    docs_dev, dlen_local = doc_kv.shape[:2]
    ntraj, cites = citations.shape
    ndocs = doc_slot.shape[0]
    nown = ndocs // docs_dev
    match = citations[:, :, None] == jnp.arange(ndocs, dtype=jnp.int32)[None, None, :]
    slots = jnp.sum(jnp.where(match, doc_slot[None, None, :], 0), -1)
    to_owner = (slots // docs_dev)[:, :, None] == jnp.arange(nown, dtype=jnp.int32)[None, None, :]
    local = jnp.max(jnp.where(to_owner, (slots % docs_dev)[:, :, None], -1), 1)
    local = local.reshape(NX, NZ, NC, NX, NZ, NC)
    hot = lambda i, n: jnp.arange(n, dtype=jnp.int32) == i
    isx, isz, isc = hot(x, NX), hot(z, NZ), hot(c, NC)
    pick_k = (isx[:, None, None, None, None, None] & isz[None, None, None, None, :, None] & isc)
    pick_v = (isz[None, :, None, None, None, None] & isx[None, None, None, :, None, None] & isc)
    kred = jnp.sum(jnp.where(pick_k, local, 0), (0, 4, 5)).reshape(-1)
    vred = jnp.sum(jnp.where(pick_v, local, 0), (1, 3, 5)).reshape(-1)
    mine = jnp.any(to_owner & hot(me, ntraj)[:, None, None], 0)
    cite_of = jnp.sum(jnp.where(mine, jnp.arange(cites, dtype=jnp.int32)[:, None], 0), 0).reshape(NX, NZ, NC)
    own_owner = jnp.sum(jnp.where(mine, jnp.arange(nown, dtype=jnp.int32)[None, :], 0), 1)
    ox, oz, oc = own_owner // (NZ * NC), (own_owner // NC) % NZ, own_owner % NC
    pad = lambda a: jnp.pad(a, (0, nown - cites))
    tab = jnp.stack([
        pad((oz * NC + oc) * 4 + ox), pad((ox * NC + oc) * 4 + oz), pad(visible_from[0]),
        cite_of.transpose(1, 2, 0).reshape(-1), cite_of.transpose(0, 2, 1).reshape(-1), kred, vred])
    own = doc_kv.reshape(docs_dev, dlen_local, NY, kv_local, 2, hdim).transpose(2, 3, 4, 0, 1, 5)
    split = (tlen, kv_local, group, hdim)
    attended, d_queries, d_traj, d_doc = attention(
        tab, queries.reshape(split), grad_out.reshape(split), traj_kv.reshape(tlen, kv_local * 2 * hdim), own)
    return (attended.reshape(queries.shape), d_queries.reshape(queries.shape), d_traj.reshape(traj_kv.shape),
            d_doc.transpose(3, 4, 0, 1, 2, 5).reshape(doc_kv.shape))


def solution(mesh):
    in_specs = (
        P("dp", "head", None),
        P("dp", "head", None, None),
        P("dp", "head", None),
        P("dp", "head", None, None, None),
        P(),
        P(),
        P("dp", None),
    )
    out_specs = (
        P("dp", "head", None),
        P("dp", "head", None),
        P("dp", "head", None, None),
        P("dp", "head", None, None, None),
    )
    return jax.shard_map(body, mesh=mesh, in_specs=in_specs, out_specs=out_specs, check_vma=False)
```

```python
import functools
import math

import jax
import jax.numpy as jnp
from jax import lax
from jax.experimental import pallas as pl
from jax.experimental.pallas import tpu as pltpu
from jax.sharding import PartitionSpec as P

SEG = 64
BIG = 3.0e38
NT = (((1,), (1,)), ((), ()))
NN = (((1,), (0,)), ((), ()))
NX, NZ, NC, NY = 4, 4, 2, 4
FAR = (2, 1, 3)
f32 = jnp.float32
bf16 = jnp.bfloat16


def kernel(cit, slot_of, vis, q_hbm, g_hbm, kv_ref, own_ref, o_hbm, dq_hbm, dkv_ref, dd_ref, *scratch):
    (tab, q_ref, g_ref, o_ref, dq_ref, move) = scratch[:6]
    (qs, gs, gn, gt, ks, vs, kt, vt, sc, pp, ds, dk, dv, inv, delta) = scratch[6:21]
    bufs = scratch[21:]
    st, rowa, rowb, senda, sendb, recva, recvb, backa, backb, suma, sumb, tot, home = (
        bufs[4 * i : 4 * i + 4] for i in range(13)
    )
    sems = bufs[52:]
    me, y = lax.axis_index("dp"), lax.axis_index("head")
    x, z, c = me // (NZ * NC), (me // NC) % NZ, me % NC
    tlen, nkv, group, hdim = q_ref.shape
    dlen = st[0].shape[1]
    cites = cit.shape[1]
    ndoc = cites * dlen
    rows = SEG * group
    nseg = tlen // SEG
    nch = ndoc // (2 * dlen)
    scale = 1.0 / math.sqrt(hdim)
    c1 = scale * math.log2(math.e)
    part = dlen // NY
    top, low = slice(0, dlen // 2), slice(dlen // 2, dlen)
    AIDX, BIDX, OWNER, ACITE, BCITE, ARED, BRED = range(7)

    def at(dx, dz, dc, dy):
        dp = (((x + dx) % NX) * NZ + (z + dz) % NZ) * NC + (c + dc) % NC
        return (dp, (y + dy) % NY)

    def copy(stage, k, i, src, dst, to):
        return pltpu.make_async_remote_copy(
            src_ref=src, dst_ref=dst, send_sem=sems[2 * stage].at[k, i], recv_sem=sems[2 * stage + 1].at[k, i],
            device_id=at(*to), device_id_type=pl.DeviceIdType.MESH)

    def tokens_of(i):
        return pl.ds(pl.multiple_of(i * part, part), part)

    def heads_out(k):
        return [copy(0, k, i, own_ref.at[(y + dy) % NY, k], st[k].at[:, tokens_of(y), :], (0, 0, 0, dy))
                for i, dy in enumerate(FAR)]

    def lines_out(k):
        a = [copy(1, k, i, st[k].at[:, top, :], rowa[k].at[pl.ds(x * 4, 4)], (d, 0, 0, 0)) for i, d in enumerate(FAR)]
        b = [copy(1, k, 3 + i, st[k].at[:, low, :], rowb[k].at[pl.ds(z * 4, 4)], (0, d, 0, 0)) for i, d in enumerate(FAR)]
        return [r for ab in zip(a, b) for r in ab]

    def cross(stage, k, dsta, dstb):
        hops = [(d, dc) for d in FAR for dc in range(NC)] + [(0, 1)]
        res = []
        for i, (d, dc) in enumerate(hops):
            other = (c + dc) % NC
            ja = ((z + d) % NZ) * NC + other
            jb = ((x + d) % NX) * NC + other
            res.append(copy(stage, k, i, senda[k].at[pl.ds(ja * 4, 4)], dsta[k].at[pl.ds((z * NC + c) * 4, 4)], (0, d, dc, 0)))
            res.append(copy(stage, k, 7 + i, sendb[k].at[pl.ds(jb * 4, 4)], dstb[k].at[pl.ds((x * NC + c) * 4, 4)], (d, 0, dc, 0)))
        return res

    def docs_out(k):
        return cross(2, k, recva, recvb)

    def grads_out(k):
        return cross(3, k, backa, backb)

    def sums_out(k):
        a = [copy(4, k, i, rowa[k].at[pl.ds((x + d) % NX * 4, 4)], suma[k].at[pl.ds(x * 4, 4)], (d, 0, 0, 0))
             for i, d in enumerate(FAR)]
        b = [copy(4, k, 3 + i, rowb[k].at[pl.ds((z + d) % NZ * 4, 4)], sumb[k].at[pl.ds(z * 4, 4)], (0, d, 0, 0))
             for i, d in enumerate(FAR)]
        return [r for ab in zip(a, b) for r in ab]

    def heads_home(k):
        return [copy(5, k, i, tot[k].at[:, tokens_of((y + dy) % NY), :], home[k].at[y], (0, 0, 0, dy))
                for i, dy in enumerate(FAR)]

    def start(copies):
        for r in copies:
            r.start()

    def wait(copies):
        for r in copies:
            r.wait()

    def send_lines(k):
        wait(heads_out(k))
        start(lines_out(k))
        rowa[k][pl.ds(x * 4, 4)] = st[k][:, top, :]
        rowb[k][pl.ds(z * 4, 4)] = st[k][:, low, :]

    def keep(k, dsta, dstb):
        ja, jb = (z * NC + c) * 4, (x * NC + c) * 4
        dsta[k][pl.ds(ja, 4)] = senda[k][pl.ds(ja, 4)]
        dstb[k][pl.ds(jb, 4)] = sendb[k][pl.ds(jb, 4)]

    def send_docs(k):
        wait(lines_out(k))

        @pl.loop(0, 32)
        def _(j):
            senda[k][j] = rowa[k][j % 4 * 4 + jnp.maximum(tab[ARED, j], 0)]
            sendb[k][j] = rowb[k][j % 4 * 4 + jnp.maximum(tab[BRED, j], 0)]

        start(docs_out(k))
        keep(k, recva, recvb)

    def gather(k, dst, dst_t):
        wait(docs_out(k))

        @pl.loop(0, cites)
        def _(i):
            a = recva[k][tab[AIDX, i]]
            b = recvb[k][tab[BIDX, i]]
            dst[pl.ds(pl.multiple_of(i * dlen, dlen), dlen // 2), :] = a
            dst[pl.ds(pl.multiple_of(i * dlen + dlen // 2, dlen // 2), dlen // 2), :] = b
            r = pl.ds(pl.multiple_of(i * dlen, dlen), dlen)
            dst_t[:, r] = dst[r, :].T

    def send_grads(k, src, factor):
        @pl.loop(0, 32)
        def _(j):
            senda[k][j] = (src[tab[ACITE, j]][top] * factor).astype(bf16)
            sendb[k][j] = (src[tab[BCITE, j]][low] * factor).astype(bf16)

        start(grads_out(k))
        keep(k, backa, backb)

    def send_sums(k):
        wait(grads_out(k))
        for back, row, red in ((backa, rowa, ARED), (backb, rowb, BRED)):
            @pl.loop(0, 4)
            def _(o):
                acc = [jnp.zeros((dlen // 2, hdim), f32)] * 4
                for t in range(8):
                    blk = back[k][t * 4 + o].astype(f32)
                    w = tab[red, t * 4 + o]
                    for d in range(4):
                        acc[d] = acc[d] + blk * jnp.where(w == d, 1.0, 0.0)
                for d in range(4):
                    row[k][o * 4 + d] = acc[d].astype(bf16)

        start(sums_out(k))
        suma[k][pl.ds(x * 4, 4)] = rowa[k][pl.ds(x * 4, 4)]
        sumb[k][pl.ds(z * 4, 4)] = rowb[k][pl.ds(z * 4, 4)]

    def send_home(k):
        wait(sums_out(k))
        for half, s in ((top, suma), (low, sumb)):
            for d in range(4):
                tot[k][d, half] = (s[k][d].astype(f32) + s[k][4 + d].astype(f32)
                                   + s[k][8 + d].astype(f32) + s[k][12 + d].astype(f32)).astype(bf16)
        start(heads_home(k))
        home[k][y] = tot[k][:, tokens_of(y), :]

    def finish(k):
        wait(heads_home(k))
        for i in range(NY):
            dd_ref[pl.ds(i * 4 + k, 4 * part, stride=4 * NY), :] = home[k][i].reshape(4 * part, hdim).astype(f32)

    def loads():
        return [pltpu.make_async_copy(q_hbm, q_ref, move.at[0]), pltpu.make_async_copy(g_hbm, g_ref, move.at[1])]

    def store(i, g):
        src, dst = ((o_ref, o_hbm), (dq_ref, dq_hbm))[i]
        return pltpu.make_async_copy(src.at[:, g], dst.at[:, g], move.at[2 + 2 * i + g])

    def tables():
        def pair(v):
            return (v >> 2) & 7

        for i in range(cites):
            v = slot_of[cit[me, i]]
            tab[OWNER, i] = v >> 2
            tab[AIDX, i] = pair(v) * 4 + (v >> 5)
            tab[BIDX, i] = ((v >> 5) * 2 + ((v >> 2) & 1)) * 4 + ((v >> 3) & 3)

        @pl.loop(0, 8)
        def _(t):
            a = [jnp.int32(-1)] * 4
            b = [jnp.int32(-1)] * 4
            for i in range(cites):
                v = slot_of[cit[x * 8 + t, i]]
                to = jnp.where(pair(v) == z * NC + c, v >> 5, -1)
                u = slot_of[cit[t // 2 * 8 + z * NC + t % 2, i]]
                uo = jnp.where(((u >> 5) == x) & (((u >> 2) & 1) == c), (u >> 3) & 3, -1)
                for o in range(4):
                    a[o] = jnp.where(to == o, v & 3, a[o])
                    b[o] = jnp.where(uo == o, u & 3, b[o])
            for o in range(4):
                tab[ARED, t * 4 + o] = a[o]
                tab[BRED, t * 4 + o] = b[o]

        @pl.loop(0, 32)
        def _(j):
            a, b = jnp.int32(0), jnp.int32(0)
            for i in range(cites):
                v = tab[OWNER, i]
                a = jnp.where(v == j % 4 * 8 + j // 4, i, a)
                b = jnp.where(v == j // 8 * 8 + j % 4 * 2 + j // 4 % 2, i, b)
            tab[ACITE, j] = a
            tab[BCITE, j] = b

    start(loads())
    barrier = pltpu.get_barrier_semaphore()
    near = [(d, 0, dc, 0) for d in range(NX) for dc in range(NC) if d or dc]
    near += [(0, d, dc, 0) for d in FAR for dc in range(NC)] + [(0, 0, 0, d) for d in FAR]
    for to in near:
        pl.semaphore_signal(barrier, inc=1, device_id=at(*to), device_id_type=pl.DeviceIdType.MESH)
    pl.semaphore_wait(barrier, len(near))

    def send_heads(k):
        start(heads_out(k))
        st[k][:, tokens_of(y), :] = own_ref[y, k]

    def prepare(g):
        half = slice(g * 2 * hdim, (g + 1) * 2 * hdim)
        qs[...] = q_ref[:, g].astype(f32).reshape(tlen * group, hdim).astype(bf16)
        gs[...] = g_ref[:, g].astype(f32).reshape(tlen * group, hdim)
        own = kv_ref[:, half]
        ks[ndoc:, :] = own[:, :hdim]
        vs[ndoc:, :] = own[:, hdim:]
        kt[:, ndoc:] = own[:, :hdim].T
        vt[:, ndoc:] = own[:, hdim:].T

    send_heads(0)
    send_heads(1)
    tables()
    send_lines(0)
    send_heads(2)
    send_heads(3)
    wait(loads())
    prepare(0)
    send_docs(0)
    send_lines(1)

    @pl.loop(0, nkv)
    def _(g):
        half = pl.ds(pl.multiple_of(g * 2 * hdim, 2 * hdim), 2 * hdim)

        def second_head():
            prepare(1)
            gather(2, ks, kt)

        pl.when(g == 0)(lambda: gather(0, ks, kt))
        pl.when(g == 1)(second_head)

        @pl.loop(0, nseg)
        def _(s):
            pl.when((g == 0) & (s == 1))(lambda: send_docs(1))
            pl.when((g == 0) & (s == 3))(lambda: send_lines(2))
            rs = pl.ds(pl.multiple_of(s * rows, rows), rows)
            q = qs[rs, :]
            m = jnp.full((8, rows), -BIG, f32)
            for i in range(nch + 1):
                r = slice(i * 2 * dlen, (i + 1) * 2 * dlen)
                score = lax.dot_general(ks[r, :], q, NT, preferred_element_type=f32)
                if i == nch:
                    key = lax.broadcasted_iota(jnp.int32, (tlen, rows), 0)
                    tok = s * SEG + lax.broadcasted_iota(jnp.int32, (tlen, rows), 1) // group
                    score = jnp.where(key <= tok, score, -BIG)
                    m = jnp.maximum(m, jnp.max(score.reshape(tlen // 8, 8, rows), axis=0))
                else:
                    for h in range(2):
                        t = jnp.max(score[h * dlen : (h + 1) * dlen].reshape(dlen // 8, 8, rows), axis=0)
                        m = jnp.maximum(m, jnp.where(s >= vis[0, 2 * i + h], t, -BIG))
                sc[r, :] = score
            m = jnp.max(m, axis=0, keepdims=True)
            total = jnp.zeros((8, rows), f32)
            for i in range(2 * nch + 2):
                r = slice(i * dlen, (i + 1) * dlen)
                mm = m if i >= 2 * nch else jnp.where(s >= vis[0, i], m, BIG)
                p = jnp.exp2((sc[r, :] - mm) * c1)
                total = total + jnp.sum(p.reshape(dlen // 8, 8, rows), axis=0)
                pp[r, rs] = p.astype(bf16)
            inv[s] = 1.0 / jnp.sum(total, axis=0, keepdims=True)

        def more_docs():
            gather(1, vs, vt)
            send_lines(3)

        pl.when(g == 0)(more_docs)
        pl.when(g == 1)(lambda: gather(3, vs, vt))

        @pl.loop(0, nseg)
        def _(s):
            rs = pl.ds(pl.multiple_of(s * rows, rows), rows)
            block = pl.ds(pl.multiple_of(s * SEG, SEG), SEG)
            ot = lax.dot_general(vt[...], pp[:, rs], NN, preferred_element_type=f32)
            ot = (ot * inv[s]).astype(bf16).astype(f32)
            o_ref[block, g] = ot.T.reshape(SEG, group, hdim).astype(bf16)
            gf = gs[rs, :].T
            delta[s] = jnp.sum(ot * gf, axis=0, keepdims=True) * inv[s]
            gf = gf * inv[s]
            gn[rs, :] = gf.T.astype(bf16)
            gt[:, rs] = gf.astype(bf16)

        def contract(dst, a, b):
            @pl.loop(0, (nch + 1) // 3)
            def _(i):
                r = pl.ds(pl.multiple_of(i * 6 * dlen, 6 * dlen), 6 * dlen)
                t = lax.dot_general(a[r, :], b[...], NN, preferred_element_type=f32)
                dst[pl.ds(i * 6, 6)] = t.reshape(6, dlen, hdim)

        def first_back():
            send_sums(1)
            send_sums(0)

        pl.when(g == 0)(lambda: store(0, 0).start())
        pl.when(g == 1)(lambda: store(0, 1).start())
        pl.when(g == 0)(lambda: send_docs(2))
        pl.when(g == 1)(first_back)
        contract(dv, pp, gn)
        pl.when(g == 0)(lambda: send_docs(3))
        pl.when(g == 1)(lambda: send_grads(3, dv, 1.0))

        @pl.loop(0, nseg)
        def _(s):
            rs = pl.ds(pl.multiple_of(s * rows, rows), rows)
            block = pl.ds(pl.multiple_of(s * SEG, SEG), SEG)
            for i in range(nch + 1):
                r = slice(i * 2 * dlen, (i + 1) * 2 * dlen)
                dp = lax.dot_general(vs[r, :], gt[:, rs], NN, preferred_element_type=f32)
                ds[r, rs] = pp[r, rs] * (dp - delta[s]).astype(bf16)
            dqt = lax.dot_general(kt[...], ds[:, rs], NN, preferred_element_type=f32) * scale
            dq_ref[block, g] = dqt.T.reshape(SEG, group, hdim).astype(bf16)

        pl.when(g == 0)(lambda: store(1, 0).start())
        pl.when(g == 1)(lambda: store(1, 1).start())
        contract(dk, ds, qs)

        def first_grads():
            send_grads(1, dv, 1.0)
            send_grads(0, dk, scale)

        pl.when(g == 0)(first_grads)
        pl.when(g == 1)(lambda: send_grads(2, dk, scale))
        own_k = dk[cites:].reshape(tlen, hdim) * scale
        dkv_ref[:, half] = jnp.concatenate([own_k, dv[cites:].reshape(tlen, hdim)], axis=1).astype(bf16)

    send_home(1)
    send_home(0)
    send_sums(3)
    finish(1)
    finish(0)
    send_sums(2)
    send_home(3)
    send_home(2)
    wait([store(i, g) for i in range(2) for g in range(2)])
    finish(3)
    finish(2)


def attention(cit, slot_of, vis, q4, g4, kv, own):
    tlen, nkv, group, hdim = q4.shape
    dlen = own.shape[0] * own.shape[3]
    cites = cit.shape[1]
    keys = cites * dlen + tlen
    nseg, rows, all_rows = tlen // SEG, SEG * group, tlen * group
    macs = all_rows * keys * hdim * nkv

    def vmem(shape, dtype=bf16):
        return pltpu.VMEM(shape, dtype)

    scratch = [pltpu.SMEM((7, 32), jnp.int32)] + [vmem(q4.shape)] * 4 + [pltpu.SemaphoreType.DMA((6,))]
    scratch += [
        vmem((all_rows, hdim)), vmem((all_rows, hdim), f32), vmem((all_rows, hdim)), vmem((hdim, all_rows)),
        vmem((keys, hdim)), vmem((keys, hdim)), vmem((hdim, keys)), vmem((hdim, keys)),
        vmem((keys, rows), f32), vmem((keys, all_rows)), vmem((keys, all_rows)),
        vmem((keys // dlen, dlen, hdim), f32), vmem((keys // dlen, dlen, hdim), f32),
        vmem((nseg, 1, rows), f32), vmem((nseg, 1, rows), f32),
    ]
    scratch += [vmem((4, dlen, hdim))] * 4
    for n in (16, 16, 32, 32, 32, 32, 32, 32, 16, 16):
        scratch += [vmem((n, dlen // 2, hdim))] * 4
    scratch += [vmem((4, dlen, hdim))] * 4
    scratch += [vmem((NY, 4, dlen // NY, hdim))] * 4
    for n in (3, 6, 14, 14, 6, 3):
        scratch += [pltpu.SemaphoreType.DMA((4, n))] * 2
    whole = pl.BlockSpec(memory_space=pltpu.VMEM)
    return pl.pallas_call(
        kernel,
        out_shape=(jax.ShapeDtypeStruct(q4.shape, bf16), jax.ShapeDtypeStruct(q4.shape, bf16),
                   jax.ShapeDtypeStruct(kv.shape, bf16), jax.ShapeDtypeStruct((own.size // hdim, hdim), f32)),
        in_specs=[pl.BlockSpec(memory_space=pltpu.SMEM)] * 3 + [pl.BlockSpec(memory_space=pl.ANY)] * 2 + [whole] * 2,
        out_specs=(pl.BlockSpec(memory_space=pl.ANY),) * 2 + (whole,) * 2,
        scratch_shapes=scratch,
        compiler_params=pltpu.CompilerParams(
            collective_id=0, has_side_effects=True, vmem_limit_bytes=67043328),
        cost_estimate=pl.CostEstimate(flops=12 * macs, bytes_accessed=8 << 20, transcendentals=macs // hdim),
        name="attention",
    )(cit, slot_of, vis, q4, g4, kv, own)


def body(queries, traj_kv, grad_out, doc_kv, citations, doc_slot, visible_from):
    tlen, heads_local, hdim = queries.shape
    kv_local = traj_kv.shape[1]
    group = heads_local // kv_local
    docs_dev, dlen_local = doc_kv.shape[:2]
    own = doc_kv.reshape(docs_dev, dlen_local, NY, kv_local, 2, hdim).transpose(2, 3, 4, 0, 1, 5)
    own = own.reshape(NY, 2 * kv_local, docs_dev, dlen_local, hdim)
    split = (tlen, kv_local, group, hdim)
    attended, d_queries, d_traj, d_doc = attention(
        citations, doc_slot, visible_from, queries.reshape(split), grad_out.reshape(split), traj_kv.reshape(tlen, kv_local * 2 * hdim), own)
    return (attended.reshape(queries.shape), d_queries.reshape(queries.shape), d_traj.reshape(traj_kv.shape),
            d_doc.reshape(doc_kv.shape))


def solution(mesh):
    in_specs = (
        P("dp", "head", None),
        P("dp", "head", None, None),
        P("dp", "head", None),
        P("dp", "head", None, None, None),
        P(),
        P(),
        P("dp", None),
    )
    out_specs = (
        P("dp", "head", None),
        P("dp", "head", None),
        P("dp", "head", None, None),
        P("dp", "head", None, None, None),
    )
    return jax.shard_map(body, mesh=mesh, in_specs=in_specs, out_specs=out_specs, check_vma=False)
```

```python
import functools
import math

import jax
import jax.numpy as jnp
from jax import lax
from jax.experimental import pallas as pl
from jax.experimental.pallas import tpu as pltpu
from jax.sharding import PartitionSpec as P

SEG = 64
BIG = 3.0e38
NT = (((1,), (1,)), ((), ()))
NN = (((1,), (0,)), ((), ()))
NX, NZ, NC, NY = 4, 4, 2, 4
FAR = (2, 1, 3)
f32 = jnp.float32
bf16 = jnp.bfloat16


def kernel(cit, slot_of, vis, q_hbm, g_hbm, kv_ref, own_ref, o_hbm, dq_hbm, dkv_ref, dd_ref, *scratch):
    (tab, q_ref, g_ref, o_ref, dq_ref, move) = scratch[:6]
    (qs, gs, gn, gt, ks, vs, kt, vt, sc, pp, ds, dk, dv, inv, delta) = scratch[6:21]
    bufs = scratch[21:]
    st, rowa, rowb, senda, sendb, recva, recvb, backa, backb, suma, sumb, tot, home = (
        bufs[4 * i : 4 * i + 4] for i in range(13)
    )
    sems = bufs[52:]
    me, y = lax.axis_index("dp"), lax.axis_index("head")
    x, z, c = me // (NZ * NC), (me // NC) % NZ, me % NC
    tlen, nkv, group, hdim = q_ref.shape
    dlen = st[0].shape[1]
    cites = cit.shape[0]
    ndoc = cites * dlen
    rows = SEG * group
    nseg = tlen // SEG
    nch = ndoc // (2 * dlen)
    scale = 1.0 / math.sqrt(hdim)
    c1 = scale * math.log2(math.e)
    part = dlen // NY
    top, low = slice(0, dlen // 2), slice(dlen // 2, dlen)
    AIDX, BIDX, OWNER, ACITE, BCITE, ARED, BRED = range(7)

    def at(dx, dz, dc, dy):
        dp = (((x + dx) % NX) * NZ + (z + dz) % NZ) * NC + (c + dc) % NC
        return (dp, (y + dy) % NY)

    def copy(stage, k, i, src, dst, to):
        return pltpu.make_async_remote_copy(
            src_ref=src, dst_ref=dst, send_sem=sems[2 * stage].at[k, i], recv_sem=sems[2 * stage + 1].at[k, i],
            device_id=at(*to), device_id_type=pl.DeviceIdType.MESH)

    def tokens_of(i):
        return pl.ds(pl.multiple_of(i * part, part), part)

    def heads_out(k):
        return [copy(0, k, i, own_ref.at[(y + dy) % NY, k], st[k].at[:, tokens_of(y), :], (0, 0, 0, dy))
                for i, dy in enumerate(FAR)]

    def lines_out(k):
        a = [copy(1, k, i, st[k].at[:, top, :], rowa[k].at[pl.ds(x * 4, 4)], (d, 0, 0, 0)) for i, d in enumerate(FAR)]
        b = [copy(1, k, 3 + i, st[k].at[:, low, :], rowb[k].at[pl.ds(z * 4, 4)], (0, d, 0, 0)) for i, d in enumerate(FAR)]
        return [r for ab in zip(a, b) for r in ab]

    def cross(stage, k, dsta, dstb):
        hops = [(d, dc) for d in FAR for dc in range(NC)] + [(0, 1)]
        res = []
        for i, (d, dc) in enumerate(hops):
            other = (c + dc) % NC
            ja = ((z + d) % NZ) * NC + other
            jb = ((x + d) % NX) * NC + other
            res.append(copy(stage, k, i, senda[k].at[pl.ds(ja * 4, 4)], dsta[k].at[pl.ds((z * NC + c) * 4, 4)], (0, d, dc, 0)))
            res.append(copy(stage, k, 7 + i, sendb[k].at[pl.ds(jb * 4, 4)], dstb[k].at[pl.ds((x * NC + c) * 4, 4)], (d, 0, dc, 0)))
        return res

    def docs_out(k):
        return cross(2, k, recva, recvb)

    def grads_out(k):
        return cross(3, k, backa, backb)

    def sums_out(k):
        a = [copy(4, k, i, rowa[k].at[pl.ds((x + d) % NX * 4, 4)], suma[k].at[pl.ds(x * 4, 4)], (d, 0, 0, 0))
             for i, d in enumerate(FAR)]
        b = [copy(4, k, 3 + i, rowb[k].at[pl.ds((z + d) % NZ * 4, 4)], sumb[k].at[pl.ds(z * 4, 4)], (0, d, 0, 0))
             for i, d in enumerate(FAR)]
        return [r for ab in zip(a, b) for r in ab]

    def heads_home(k):
        return [copy(5, k, i, tot[k].at[:, tokens_of((y + dy) % NY), :], home[k].at[y], (0, 0, 0, dy))
                for i, dy in enumerate(FAR)]

    def start(copies):
        for r in copies:
            r.start()

    def wait(copies):
        for r in copies:
            r.wait()

    def send_lines(k):
        wait(heads_out(k))
        start(lines_out(k))
        rowa[k][pl.ds(x * 4, 4)] = st[k][:, top, :]
        rowb[k][pl.ds(z * 4, 4)] = st[k][:, low, :]

    def keep(k, dsta, dstb):
        ja, jb = (z * NC + c) * 4, (x * NC + c) * 4
        dsta[k][pl.ds(ja, 4)] = senda[k][pl.ds(ja, 4)]
        dstb[k][pl.ds(jb, 4)] = sendb[k][pl.ds(jb, 4)]

    def send_docs(k):
        wait(lines_out(k))

        @pl.loop(0, 32)
        def _(j):
            senda[k][j] = rowa[k][j % 4 * 4 + jnp.maximum(tab[ARED, j], 0)]
            sendb[k][j] = rowb[k][j % 4 * 4 + jnp.maximum(tab[BRED, j], 0)]

        start(docs_out(k))
        keep(k, recva, recvb)

    def gather(k, dst, dst_t):
        wait(docs_out(k))

        @pl.loop(0, cites)
        def _(i):
            a = recva[k][tab[AIDX, i]]
            b = recvb[k][tab[BIDX, i]]
            dst[pl.ds(pl.multiple_of(i * dlen, dlen), dlen // 2), :] = a
            dst[pl.ds(pl.multiple_of(i * dlen + dlen // 2, dlen // 2), dlen // 2), :] = b
            r = pl.ds(pl.multiple_of(i * dlen, dlen), dlen)
            dst_t[:, r] = dst[r, :].T

    def send_grads(k, src, factor):
        @pl.loop(0, 32)
        def _(j):
            senda[k][j] = (src[tab[ACITE, j]][top] * factor).astype(bf16)
            sendb[k][j] = (src[tab[BCITE, j]][low] * factor).astype(bf16)

        start(grads_out(k))
        keep(k, backa, backb)

    def send_sums(k):
        wait(grads_out(k))
        for back, row, red in ((backa, rowa, ARED), (backb, rowb, BRED)):
            @pl.loop(0, 4)
            def _(o):
                acc = [jnp.zeros((dlen // 2, hdim), f32)] * 4
                for t in range(8):
                    blk = back[k][t * 4 + o].astype(f32)
                    w = tab[red, t * 4 + o]
                    for d in range(4):
                        acc[d] = acc[d] + blk * jnp.where(w == d, 1.0, 0.0)
                for d in range(4):
                    row[k][o * 4 + d] = acc[d].astype(bf16)

        start(sums_out(k))
        suma[k][pl.ds(x * 4, 4)] = rowa[k][pl.ds(x * 4, 4)]
        sumb[k][pl.ds(z * 4, 4)] = rowb[k][pl.ds(z * 4, 4)]

    def send_home(k):
        wait(sums_out(k))
        for half, s in ((top, suma), (low, sumb)):
            for d in range(4):
                tot[k][d, half] = (s[k][d].astype(f32) + s[k][4 + d].astype(f32)
                                   + s[k][8 + d].astype(f32) + s[k][12 + d].astype(f32)).astype(bf16)
        start(heads_home(k))
        home[k][y] = tot[k][:, tokens_of(y), :]

    def finish(k):
        wait(heads_home(k))
        for i in range(NY):
            dd_ref[pl.ds(i * 4 + k, 4 * part, stride=4 * NY), :] = home[k][i].reshape(4 * part, hdim).astype(f32)

    def loads():
        return [pltpu.make_async_copy(q_hbm, q_ref, move.at[0]), pltpu.make_async_copy(g_hbm, g_ref, move.at[1])]

    def store(i, g):
        src, dst = ((o_ref, o_hbm), (dq_ref, dq_hbm))[i]
        return pltpu.make_async_copy(src.at[:, g], dst.at[:, g], move.at[2 + 2 * i + g])

    def tables():
        def pair(v):
            return (v >> 2) & 7

        for i in range(cites):
            v = slot_of[cit[i, me]]
            tab[OWNER, i] = v >> 2
            tab[AIDX, i] = pair(v) * 4 + (v >> 5)
            tab[BIDX, i] = ((v >> 5) * 2 + ((v >> 2) & 1)) * 4 + ((v >> 3) & 3)

        @pl.loop(0, 8)
        def _(t):
            a = [jnp.int32(-1)] * 4
            b = [jnp.int32(-1)] * 4
            for i in range(cites):
                v = slot_of[cit[i, x * 8 + t]]
                to = jnp.where(pair(v) == z * NC + c, v >> 5, -1)
                u = slot_of[cit[i, t // 2 * 8 + z * NC + t % 2]]
                uo = jnp.where(((u >> 5) == x) & (((u >> 2) & 1) == c), (u >> 3) & 3, -1)
                for o in range(4):
                    a[o] = jnp.where(to == o, v & 3, a[o])
                    b[o] = jnp.where(uo == o, u & 3, b[o])
            for o in range(4):
                tab[ARED, t * 4 + o] = a[o]
                tab[BRED, t * 4 + o] = b[o]

        @pl.loop(0, 32)
        def _(j):
            a, b = jnp.int32(0), jnp.int32(0)
            for i in range(cites):
                v = tab[OWNER, i]
                a = jnp.where(v == j % 4 * 8 + j // 4, i, a)
                b = jnp.where(v == j // 8 * 8 + j % 4 * 2 + j // 4 % 2, i, b)
            tab[ACITE, j] = a
            tab[BCITE, j] = b

    start(loads())
    barrier = pltpu.get_barrier_semaphore()
    near = [(d, 0, dc, 0) for d in range(NX) for dc in range(NC) if d or dc]
    near += [(0, d, dc, 0) for d in FAR for dc in range(NC)] + [(0, 0, 0, d) for d in FAR]
    for to in near:
        pl.semaphore_signal(barrier, inc=1, device_id=at(*to), device_id_type=pl.DeviceIdType.MESH)
    pl.semaphore_wait(barrier, len(near))

    def send_heads(k):
        start(heads_out(k))
        st[k][:, tokens_of(y), :] = own_ref[y, k]

    def prepare(g):
        qs[...] = q_ref[:, g].astype(f32).reshape(tlen * group, hdim).astype(bf16)
        gs[...] = g_ref[:, g].astype(f32).reshape(tlen * group, hdim)
        own = kv_ref[:, g].astype(f32)
        for i, (a, b) in enumerate(((ks, kt), (vs, vt))):
            t = own[:, i].astype(bf16)
            a[ndoc:, :] = t
            b[:, ndoc:] = t.T

    send_heads(0)
    send_heads(1)
    tables()
    send_lines(0)
    send_heads(2)
    send_heads(3)
    wait(loads())
    prepare(0)
    send_docs(0)
    send_lines(1)

    @pl.loop(0, nkv)
    def _(g):
        def second_head():
            prepare(1)
            gather(2, ks, kt)

        pl.when(g == 0)(lambda: gather(0, ks, kt))
        pl.when(g == 1)(second_head)

        @pl.loop(0, nseg)
        def _(s):
            pl.when((g == 0) & (s == 1))(lambda: send_docs(1))
            pl.when((g == 0) & (s == 3))(lambda: send_lines(2))
            rs = pl.ds(pl.multiple_of(s * rows, rows), rows)
            q = qs[rs, :]
            m = jnp.full((8, rows), -BIG, f32)
            for i in range(nch + 1):
                r = slice(i * 2 * dlen, (i + 1) * 2 * dlen)
                score = lax.dot_general(ks[r, :], q, NT, preferred_element_type=f32)
                if i == nch:
                    key = lax.broadcasted_iota(jnp.int32, (tlen, rows), 0)
                    tok = s * SEG + lax.broadcasted_iota(jnp.int32, (tlen, rows), 1) // group
                    score = jnp.where(key <= tok, score, -BIG)
                    m = jnp.maximum(m, jnp.max(score.reshape(tlen // 8, 8, rows), axis=0))
                else:
                    for h in range(2):
                        t = jnp.max(score[h * dlen : (h + 1) * dlen].reshape(dlen // 8, 8, rows), axis=0)
                        m = jnp.maximum(m, jnp.where(s >= vis[0, 2 * i + h], t, -BIG))
                sc[r, :] = score
            m = jnp.max(m, axis=0, keepdims=True)
            total = jnp.zeros((8, rows), f32)
            for i in range(2 * nch + 2):
                r = slice(i * dlen, (i + 1) * dlen)
                mm = m if i >= 2 * nch else jnp.where(s >= vis[0, i], m, BIG)
                p = jnp.exp2((sc[r, :] - mm) * c1)
                total = total + jnp.sum(p.reshape(dlen // 8, 8, rows), axis=0)
                pp[r, rs] = p.astype(bf16)
            inv[s] = 1.0 / jnp.sum(total, axis=0, keepdims=True)

        def more_docs():
            gather(1, vs, vt)
            send_lines(3)

        pl.when(g == 0)(more_docs)
        pl.when(g == 1)(lambda: gather(3, vs, vt))

        @pl.loop(0, nseg)
        def _(s):
            rs = pl.ds(pl.multiple_of(s * rows, rows), rows)
            block = pl.ds(pl.multiple_of(s * SEG, SEG), SEG)
            ot = lax.dot_general(vt[...], pp[:, rs], NN, preferred_element_type=f32)
            ot = (ot * inv[s]).astype(bf16).astype(f32)
            o_ref[block, g] = ot.T.reshape(SEG, group, hdim).astype(bf16)
            gf = gs[rs, :].T
            delta[s] = jnp.sum(ot * gf, axis=0, keepdims=True) * inv[s]
            gf = gf * inv[s]
            gn[rs, :] = gf.T.astype(bf16)
            gt[:, rs] = gf.astype(bf16)

        def contract(dst, a, b):
            @pl.loop(0, (nch + 1) // 3)
            def _(i):
                r = pl.ds(pl.multiple_of(i * 6 * dlen, 6 * dlen), 6 * dlen)
                t = lax.dot_general(a[r, :], b[...], NN, preferred_element_type=f32)
                dst[pl.ds(i * 6, 6)] = t.reshape(6, dlen, hdim)

        def first_back():
            send_sums(1)
            send_sums(0)

        pl.when(g == 0)(lambda: store(0, 0).start())
        pl.when(g == 1)(lambda: store(0, 1).start())
        pl.when(g == 0)(lambda: send_docs(2))
        pl.when(g == 1)(first_back)
        contract(dv, pp, gn)
        pl.when(g == 0)(lambda: send_docs(3))
        pl.when(g == 1)(lambda: send_grads(3, dv, 1.0))

        @pl.loop(0, nseg)
        def _(s):
            rs = pl.ds(pl.multiple_of(s * rows, rows), rows)
            block = pl.ds(pl.multiple_of(s * SEG, SEG), SEG)
            for i in range(nch + 1):
                r = slice(i * 2 * dlen, (i + 1) * 2 * dlen)
                dp = lax.dot_general(vs[r, :], gt[:, rs], NN, preferred_element_type=f32)
                ds[r, rs] = pp[r, rs] * (dp - delta[s]).astype(bf16)
            dqt = lax.dot_general(kt[...], ds[:, rs], NN, preferred_element_type=f32) * scale
            dq_ref[block, g] = dqt.T.reshape(SEG, group, hdim).astype(bf16)

        pl.when(g == 0)(lambda: store(1, 0).start())
        pl.when(g == 1)(lambda: store(1, 1).start())
        contract(dk, ds, qs)

        def first_grads():
            send_grads(1, dv, 1.0)
            send_grads(0, dk, scale)

        pl.when(g == 0)(first_grads)
        pl.when(g == 1)(lambda: send_grads(2, dk, scale))
        for i, t in enumerate((dk[cites:] * scale, dv[cites:])):
            dkv_ref[:, g, i] = t.reshape(tlen, hdim).astype(bf16)

    send_home(1)
    send_home(0)
    send_sums(3)
    finish(1)
    finish(0)
    send_sums(2)
    send_home(3)
    send_home(2)
    wait([store(i, g) for i in range(2) for g in range(2)])
    finish(3)
    finish(2)


def attention(cit, slot_of, vis, q4, g4, kv, own):
    tlen, nkv, group, hdim = q4.shape
    dlen = own.shape[0] * own.shape[3]
    cites = cit.shape[0]
    keys = cites * dlen + tlen
    nseg, rows, all_rows = tlen // SEG, SEG * group, tlen * group
    macs = all_rows * keys * hdim * nkv

    def vmem(shape, dtype=bf16):
        return pltpu.VMEM(shape, dtype)

    scratch = [pltpu.SMEM((7, 32), jnp.int32)] + [vmem(q4.shape)] * 4 + [pltpu.SemaphoreType.DMA((6,))]
    scratch += [
        vmem((all_rows, hdim)), vmem((all_rows, hdim), f32), vmem((all_rows, hdim)), vmem((hdim, all_rows)),
        vmem((keys, hdim)), vmem((keys, hdim)), vmem((hdim, keys)), vmem((hdim, keys)),
        vmem((keys, rows), f32), vmem((keys, all_rows)), vmem((keys, all_rows)),
        vmem((keys // dlen, dlen, hdim), f32), vmem((keys // dlen, dlen, hdim), f32),
        vmem((nseg, 1, rows), f32), vmem((nseg, 1, rows), f32),
    ]
    scratch += [vmem((4, dlen, hdim))] * 4
    for n in (16, 16, 32, 32, 32, 32, 32, 32, 16, 16):
        scratch += [vmem((n, dlen // 2, hdim))] * 4
    scratch += [vmem((4, dlen, hdim))] * 4
    scratch += [vmem((NY, 4, dlen // NY, hdim))] * 4
    for n in (3, 6, 14, 14, 6, 3):
        scratch += [pltpu.SemaphoreType.DMA((4, n))] * 2
    whole = pl.BlockSpec(memory_space=pltpu.VMEM)
    return pl.pallas_call(
        kernel,
        out_shape=(jax.ShapeDtypeStruct(q4.shape, bf16), jax.ShapeDtypeStruct(q4.shape, bf16),
                   jax.ShapeDtypeStruct(kv.shape, bf16), jax.ShapeDtypeStruct((own.size // hdim, hdim), f32)),
        in_specs=[pl.BlockSpec(memory_space=pltpu.SMEM)] * 3 + [pl.BlockSpec(memory_space=pl.ANY)] * 2 + [whole] * 2,
        out_specs=(pl.BlockSpec(memory_space=pl.ANY),) * 2 + (whole,) * 2,
        scratch_shapes=scratch,
        compiler_params=pltpu.CompilerParams(
            collective_id=0, has_side_effects=True, vmem_limit_bytes=67043328),
        cost_estimate=pl.CostEstimate(flops=12 * macs, bytes_accessed=8 << 20, transcendentals=macs // hdim),
        name="attention",
    )(cit, slot_of, vis, q4, g4, kv, own)


def body(queries, traj_kv, grad_out, doc_kv, citations, doc_slot, visible_from):
    tlen, heads_local, hdim = queries.shape
    kv_local = traj_kv.shape[1]
    group = heads_local // kv_local
    docs_dev, dlen_local = doc_kv.shape[:2]
    own = doc_kv.reshape(docs_dev, dlen_local, NY, kv_local, 2, hdim).transpose(2, 3, 4, 0, 1, 5)
    own = own.reshape(NY, 2 * kv_local, docs_dev, dlen_local, hdim)
    split = (tlen, kv_local, group, hdim)
    attended, d_queries, d_traj, d_doc = attention(
        citations.T, doc_slot, visible_from, queries.reshape(split), grad_out.reshape(split), traj_kv, own)
    return (attended.reshape(queries.shape), d_queries.reshape(queries.shape), d_traj,
            d_doc.reshape(doc_kv.shape))


def solution(mesh):
    in_specs = (
        P("dp", "head", None),
        P("dp", "head", None, None),
        P("dp", "head", None),
        P("dp", "head", None, None, None),
        P(),
        P(),
        P("dp", None),
    )
    out_specs = (
        P("dp", "head", None),
        P("dp", "head", None),
        P("dp", "head", None, None),
        P("dp", "head", None, None, None),
    )
    return jax.shard_map(body, mesh=mesh, in_specs=in_specs, out_specs=out_specs, check_vma=False)
```

```python
import functools
import math

import jax
import jax.numpy as jnp
from jax import lax
from jax.experimental import pallas as pl
from jax.experimental.pallas import tpu as pltpu
from jax.sharding import PartitionSpec as P

SEG = 64
BIG = 3.0e38
NT = (((1,), (1,)), ((), ()))
NN = (((1,), (0,)), ((), ()))
NX, NZ, NC, NY = 4, 4, 2, 4
FAR = (2, 1, 3)
f32 = jnp.float32
bf16 = jnp.bfloat16


def kernel(cit, slot_of, vis, q_hbm, g_hbm, kv_ref, doc_ref, o_hbm, dq_hbm, dkv_ref, dd_ref, *scratch):
    (tab, q_ref, g_ref, o_ref, dq_ref, move) = scratch[:6]
    own_ref = scratch[-1]
    (qs, gs, gn, gt, ks, vs, kt, vt, sc, pp, ds, dk, dv, inv, delta) = scratch[6:21]
    bufs = scratch[21:]
    st, rowa, rowb, senda, sendb, recva, recvb, backa, backb, suma, sumb, tot, home = (
        bufs[4 * i : 4 * i + 4] for i in range(13)
    )
    sems = bufs[52:-1]
    me, y = lax.axis_index("dp"), lax.axis_index("head")
    x, z, c = me // (NZ * NC), (me // NC) % NZ, me % NC
    tlen, nkv, group, hdim = q_ref.shape
    dlen = st[0].shape[1]
    cites = cit.shape[0]
    ndoc = cites * dlen
    rows = SEG * group
    nseg = tlen // SEG
    nch = ndoc // (2 * dlen)
    scale = 1.0 / math.sqrt(hdim)
    c1 = scale * math.log2(math.e)
    part = dlen // NY
    top, low = slice(0, dlen // 2), slice(dlen // 2, dlen)
    AIDX, BIDX, OWNER, ACITE, BCITE, ARED, BRED = range(7)

    def at(dx, dz, dc, dy):
        dp = (((x + dx) % NX) * NZ + (z + dz) % NZ) * NC + (c + dc) % NC
        return (dp, (y + dy) % NY)

    def copy(stage, k, i, src, dst, to):
        return pltpu.make_async_remote_copy(
            src_ref=src, dst_ref=dst, send_sem=sems[2 * stage].at[k, i], recv_sem=sems[2 * stage + 1].at[k, i],
            device_id=at(*to), device_id_type=pl.DeviceIdType.MESH)

    def tokens_of(i):
        return pl.ds(pl.multiple_of(i * part, part), part)

    def heads_out(k):
        return [copy(0, k, i, own_ref.at[(y + dy) % NY, k], st[k].at[:, tokens_of(y), :], (0, 0, 0, dy))
                for i, dy in enumerate(FAR)]

    def lines_out(k):
        a = [copy(1, k, i, st[k].at[:, top, :], rowa[k].at[pl.ds(x * 4, 4)], (d, 0, 0, 0)) for i, d in enumerate(FAR)]
        b = [copy(1, k, 3 + i, st[k].at[:, low, :], rowb[k].at[pl.ds(z * 4, 4)], (0, d, 0, 0)) for i, d in enumerate(FAR)]
        return [r for ab in zip(a, b) for r in ab]

    def cross(stage, k, dsta, dstb):
        hops = [(d, dc) for d in FAR for dc in range(NC)] + [(0, 1)]
        res = []
        for i, (d, dc) in enumerate(hops):
            other = (c + dc) % NC
            ja = ((z + d) % NZ) * NC + other
            jb = ((x + d) % NX) * NC + other
            res.append(copy(stage, k, i, senda[k].at[pl.ds(ja * 4, 4)], dsta[k].at[pl.ds((z * NC + c) * 4, 4)], (0, d, dc, 0)))
            res.append(copy(stage, k, 7 + i, sendb[k].at[pl.ds(jb * 4, 4)], dstb[k].at[pl.ds((x * NC + c) * 4, 4)], (d, 0, dc, 0)))
        return res

    def docs_out(k):
        return cross(2, k, recva, recvb)

    def grads_out(k):
        return cross(3, k, backa, backb)

    def sums_out(k):
        a = [copy(4, k, i, rowa[k].at[pl.ds((x + d) % NX * 4, 4)], suma[k].at[pl.ds(x * 4, 4)], (d, 0, 0, 0))
             for i, d in enumerate(FAR)]
        b = [copy(4, k, 3 + i, rowb[k].at[pl.ds((z + d) % NZ * 4, 4)], sumb[k].at[pl.ds(z * 4, 4)], (0, d, 0, 0))
             for i, d in enumerate(FAR)]
        return [r for ab in zip(a, b) for r in ab]

    def heads_home(k):
        return [copy(5, k, i, tot[k].at[:, tokens_of((y + dy) % NY), :], home[k].at[y], (0, 0, 0, dy))
                for i, dy in enumerate(FAR)]

    def start(copies):
        for r in copies:
            r.start()

    def wait(copies):
        for r in copies:
            r.wait()

    def send_lines(k):
        wait(heads_out(k))
        start(lines_out(k))
        rowa[k][pl.ds(x * 4, 4)] = st[k][:, top, :]
        rowb[k][pl.ds(z * 4, 4)] = st[k][:, low, :]

    def keep(k, dsta, dstb):
        ja, jb = (z * NC + c) * 4, (x * NC + c) * 4
        dsta[k][pl.ds(ja, 4)] = senda[k][pl.ds(ja, 4)]
        dstb[k][pl.ds(jb, 4)] = sendb[k][pl.ds(jb, 4)]

    def send_docs(k):
        wait(lines_out(k))

        @pl.loop(0, 32)
        def _(j):
            senda[k][j] = rowa[k][j % 4 * 4 + jnp.maximum(tab[ARED, j], 0)]
            sendb[k][j] = rowb[k][j % 4 * 4 + jnp.maximum(tab[BRED, j], 0)]

        start(docs_out(k))
        keep(k, recva, recvb)

    def gather(k, dst, dst_t):
        wait(docs_out(k))

        @pl.loop(0, cites)
        def _(i):
            a = recva[k][tab[AIDX, i]]
            b = recvb[k][tab[BIDX, i]]
            dst[pl.ds(pl.multiple_of(i * dlen, dlen), dlen // 2), :] = a
            dst[pl.ds(pl.multiple_of(i * dlen + dlen // 2, dlen // 2), dlen // 2), :] = b
            r = pl.ds(pl.multiple_of(i * dlen, dlen), dlen)
            dst_t[:, r] = dst[r, :].T

    def send_grads(k, src, factor):
        @pl.loop(0, 32)
        def _(j):
            senda[k][j] = (src[tab[ACITE, j]][top] * factor).astype(bf16)
            sendb[k][j] = (src[tab[BCITE, j]][low] * factor).astype(bf16)

        start(grads_out(k))
        keep(k, backa, backb)

    def send_sums(k):
        wait(grads_out(k))
        for back, row, red in ((backa, rowa, ARED), (backb, rowb, BRED)):
            @pl.loop(0, 4)
            def _(o):
                acc = [jnp.zeros((dlen // 2, hdim), f32)] * 4
                for t in range(8):
                    blk = back[k][t * 4 + o].astype(f32)
                    w = tab[red, t * 4 + o]
                    for d in range(4):
                        acc[d] = acc[d] + blk * jnp.where(w == d, 1.0, 0.0)
                for d in range(4):
                    row[k][o * 4 + d] = acc[d].astype(bf16)

        start(sums_out(k))
        suma[k][pl.ds(x * 4, 4)] = rowa[k][pl.ds(x * 4, 4)]
        sumb[k][pl.ds(z * 4, 4)] = rowb[k][pl.ds(z * 4, 4)]

    def send_home(k):
        wait(sums_out(k))
        for half, s in ((top, suma), (low, sumb)):
            for d in range(4):
                tot[k][d, half] = (s[k][d].astype(f32) + s[k][4 + d].astype(f32)
                                   + s[k][8 + d].astype(f32) + s[k][12 + d].astype(f32)).astype(bf16)
        start(heads_home(k))
        home[k][y] = tot[k][:, tokens_of(y), :]

    def finish(k):
        wait(heads_home(k))
        for i in range(NY):
            dd_ref[pl.ds(i * 4 + k, 4 * part, stride=4 * NY), :] = home[k][i].reshape(4 * part, hdim).astype(f32)

    def loads():
        return [pltpu.make_async_copy(q_hbm, q_ref, move.at[0]), pltpu.make_async_copy(g_hbm, g_ref, move.at[1])]

    def store(i, g):
        src, dst = ((o_ref, o_hbm), (dq_ref, dq_hbm))[i]
        return pltpu.make_async_copy(src.at[:, g], dst.at[:, g], move.at[2 + 2 * i + g])

    def tables():
        def pair(v):
            return (v >> 2) & 7

        for i in range(cites):
            v = slot_of[cit[i, me]]
            tab[OWNER, i] = v >> 2
            tab[AIDX, i] = pair(v) * 4 + (v >> 5)
            tab[BIDX, i] = ((v >> 5) * 2 + ((v >> 2) & 1)) * 4 + ((v >> 3) & 3)

        @pl.loop(0, 8)
        def _(t):
            a = [jnp.int32(-1)] * 4
            b = [jnp.int32(-1)] * 4
            for i in range(cites):
                v = slot_of[cit[i, x * 8 + t]]
                to = jnp.where(pair(v) == z * NC + c, v >> 5, -1)
                u = slot_of[cit[i, t // 2 * 8 + z * NC + t % 2]]
                uo = jnp.where(((u >> 5) == x) & (((u >> 2) & 1) == c), (u >> 3) & 3, -1)
                for o in range(4):
                    a[o] = jnp.where(to == o, v & 3, a[o])
                    b[o] = jnp.where(uo == o, u & 3, b[o])
            for o in range(4):
                tab[ARED, t * 4 + o] = a[o]
                tab[BRED, t * 4 + o] = b[o]

        @pl.loop(0, 32)
        def _(j):
            a, b = jnp.int32(0), jnp.int32(0)
            for i in range(cites):
                v = tab[OWNER, i]
                a = jnp.where(v == j % 4 * 8 + j // 4, i, a)
                b = jnp.where(v == j // 8 * 8 + j % 4 * 2 + j // 4 % 2, i, b)
            tab[ACITE, j] = a
            tab[BCITE, j] = b

    start(loads())
    for i in range(NY * nkv):
        t = doc_ref[:, :, i].astype(f32)
        for h in range(2):
            own_ref[i // nkv, i % nkv * 2 + h] = t[:, :, h].astype(bf16)
    barrier = pltpu.get_barrier_semaphore()
    near = [(d, 0, dc, 0) for d in range(NX) for dc in range(NC) if d or dc]
    near += [(0, d, dc, 0) for d in FAR for dc in range(NC)] + [(0, 0, 0, d) for d in FAR]
    for to in near:
        pl.semaphore_signal(barrier, inc=1, device_id=at(*to), device_id_type=pl.DeviceIdType.MESH)
    pl.semaphore_wait(barrier, len(near))

    def send_heads(k):
        start(heads_out(k))
        st[k][:, tokens_of(y), :] = own_ref[y, k]

    def prepare(g):
        qs[...] = q_ref[:, g].astype(f32).reshape(tlen * group, hdim).astype(bf16)
        gs[...] = g_ref[:, g].astype(f32).reshape(tlen * group, hdim)
        own = kv_ref[:, g].astype(f32)
        for i, (a, b) in enumerate(((ks, kt), (vs, vt))):
            t = own[:, i].astype(bf16)
            a[ndoc:, :] = t
            b[:, ndoc:] = t.T

    send_heads(0)
    send_heads(1)
    tables()
    send_lines(0)
    send_heads(2)
    send_heads(3)
    wait(loads())
    prepare(0)
    send_docs(0)
    send_lines(1)

    @pl.loop(0, nkv)
    def _(g):
        def second_head():
            prepare(1)
            gather(2, ks, kt)

        pl.when(g == 0)(lambda: gather(0, ks, kt))
        pl.when(g == 1)(second_head)

        @pl.loop(0, nseg)
        def _(s):
            pl.when((g == 0) & (s == 1))(lambda: send_docs(1))
            pl.when((g == 0) & (s == 3))(lambda: send_lines(2))
            rs = pl.ds(pl.multiple_of(s * rows, rows), rows)
            q = qs[rs, :]
            m = jnp.full((8, rows), -BIG, f32)
            for i in range(nch + 1):
                r = slice(i * 2 * dlen, (i + 1) * 2 * dlen)
                score = lax.dot_general(ks[r, :], q, NT, preferred_element_type=f32)
                if i == nch:
                    key = lax.broadcasted_iota(jnp.int32, (tlen, rows), 0)
                    tok = s * SEG + lax.broadcasted_iota(jnp.int32, (tlen, rows), 1) // group
                    score = jnp.where(key <= tok, score, -BIG)
                    m = jnp.maximum(m, jnp.max(score.reshape(tlen // 8, 8, rows), axis=0))
                else:
                    for h in range(2):
                        t = jnp.max(score[h * dlen : (h + 1) * dlen].reshape(dlen // 8, 8, rows), axis=0)
                        m = jnp.maximum(m, jnp.where(s >= vis[0, 2 * i + h], t, -BIG))
                sc[r, :] = score
            m = jnp.max(m, axis=0, keepdims=True)
            total = jnp.zeros((8, rows), f32)
            for i in range(2 * nch + 2):
                r = slice(i * dlen, (i + 1) * dlen)
                mm = m if i >= 2 * nch else jnp.where(s >= vis[0, i], m, BIG)
                p = jnp.exp2((sc[r, :] - mm) * c1)
                total = total + jnp.sum(p.reshape(dlen // 8, 8, rows), axis=0)
                pp[r, rs] = p.astype(bf16)
            inv[s] = 1.0 / jnp.sum(total, axis=0, keepdims=True)

        def more_docs():
            gather(1, vs, vt)
            send_lines(3)

        pl.when(g == 0)(more_docs)
        pl.when(g == 1)(lambda: gather(3, vs, vt))
        pl.when(g == 1)(lambda: send_sums(1))

        @pl.loop(0, nseg)
        def _(s):
            rs = pl.ds(pl.multiple_of(s * rows, rows), rows)
            block = pl.ds(pl.multiple_of(s * SEG, SEG), SEG)
            ot = lax.dot_general(vt[...], pp[:, rs], NN, preferred_element_type=f32)
            ot = (ot * inv[s]).astype(bf16).astype(f32)
            o_ref[block, g] = ot.T.reshape(SEG, group, hdim).astype(bf16)
            gf = gs[rs, :].T
            delta[s] = jnp.sum(ot * gf, axis=0, keepdims=True) * inv[s]
            gf = gf * inv[s]
            gn[rs, :] = gf.T.astype(bf16)
            gt[:, rs] = gf.astype(bf16)

        def contract(dst, a, b):
            @pl.loop(0, (nch + 1) // 3)
            def _(i):
                r = pl.ds(pl.multiple_of(i * 6 * dlen, 6 * dlen), 6 * dlen)
                t = lax.dot_general(a[r, :], b[...], NN, preferred_element_type=f32)
                dst[pl.ds(i * 6, 6)] = t.reshape(6, dlen, hdim)

        def first_back():
            send_sums(0)

        pl.when(g == 0)(lambda: store(0, 0).start())
        pl.when(g == 1)(lambda: store(0, 1).start())
        pl.when(g == 0)(lambda: send_docs(2))
        pl.when(g == 1)(first_back)
        contract(dv, pp, gn)
        pl.when(g == 0)(lambda: send_docs(3))
        pl.when(g == 0)(lambda: send_grads(1, dv, 1.0))
        pl.when(g == 1)(lambda: send_grads(3, dv, 1.0))

        @pl.loop(0, nseg)
        def _(s):
            rs = pl.ds(pl.multiple_of(s * rows, rows), rows)
            block = pl.ds(pl.multiple_of(s * SEG, SEG), SEG)
            for i in range(nch + 1):
                r = slice(i * 2 * dlen, (i + 1) * 2 * dlen)
                dp = lax.dot_general(vs[r, :], gt[:, rs], NN, preferred_element_type=f32)
                ds[r, rs] = pp[r, rs] * (dp - delta[s]).astype(bf16)
            dqt = lax.dot_general(kt[...], ds[:, rs], NN, preferred_element_type=f32) * scale
            dq_ref[block, g] = dqt.T.reshape(SEG, group, hdim).astype(bf16)

        pl.when(g == 0)(lambda: store(1, 0).start())
        pl.when(g == 1)(lambda: store(1, 1).start())
        contract(dk, ds, qs)

        def first_grads():
            send_grads(0, dk, scale)

        pl.when(g == 0)(first_grads)
        pl.when(g == 1)(lambda: send_grads(2, dk, scale))
        for i, t in enumerate((dk[cites:] * scale, dv[cites:])):
            dkv_ref[:, g, i] = t.reshape(tlen, hdim).astype(bf16)

    send_home(1)
    send_home(0)
    send_sums(3)
    finish(1)
    send_sums(2)
    send_home(3)
    finish(0)
    wait([store(i, g) for i in range(2) for g in range(2)])
    send_home(2)
    finish(3)
    finish(2)


def attention(cit, slot_of, vis, q4, g4, kv, own):
    tlen, nkv, group, hdim = q4.shape
    docs_dev, dlen_local = own.shape[:2]
    dlen = NY * dlen_local
    cites = cit.shape[0]
    keys = cites * dlen + tlen
    nseg, rows, all_rows = tlen // SEG, SEG * group, tlen * group
    macs = all_rows * keys * hdim * nkv

    def vmem(shape, dtype=bf16):
        return pltpu.VMEM(shape, dtype)

    scratch = [pltpu.SMEM((7, 32), jnp.int32)] + [vmem(q4.shape)] * 4 + [pltpu.SemaphoreType.DMA((6,))]
    scratch += [
        vmem((all_rows, hdim)), vmem((all_rows, hdim), f32), vmem((all_rows, hdim)), vmem((hdim, all_rows)),
        vmem((keys, hdim)), vmem((keys, hdim)), vmem((hdim, keys)), vmem((hdim, keys)),
        vmem((keys, rows), f32), vmem((keys, all_rows)), vmem((keys, all_rows)),
        vmem((keys // dlen, dlen, hdim), f32), vmem((keys // dlen, dlen, hdim), f32),
        vmem((nseg, 1, rows), f32), vmem((nseg, 1, rows), f32),
    ]
    scratch += [vmem((4, dlen, hdim))] * 4
    for n in (16, 16, 32, 32, 32, 32, 32, 32, 16, 16):
        scratch += [vmem((n, dlen // 2, hdim))] * 4
    scratch += [vmem((4, dlen, hdim))] * 4
    scratch += [vmem((NY, 4, dlen // NY, hdim))] * 4
    for n in (3, 6, 14, 14, 6, 3):
        scratch += [pltpu.SemaphoreType.DMA((4, n))] * 2
    scratch += [vmem((NY, 2 * nkv, docs_dev, dlen_local, hdim))]
    whole = pl.BlockSpec(memory_space=pltpu.VMEM)
    return pl.pallas_call(
        kernel,
        out_shape=(jax.ShapeDtypeStruct(q4.shape, bf16), jax.ShapeDtypeStruct(q4.shape, bf16),
                   jax.ShapeDtypeStruct(kv.shape, bf16), jax.ShapeDtypeStruct((own.size // hdim, hdim), f32)),
        in_specs=[pl.BlockSpec(memory_space=pltpu.SMEM)] * 3 + [pl.BlockSpec(memory_space=pl.ANY)] * 2 + [whole] * 2,
        out_specs=(pl.BlockSpec(memory_space=pl.ANY),) * 2 + (whole,) * 2,
        scratch_shapes=scratch,
        compiler_params=pltpu.CompilerParams(
            collective_id=0, has_side_effects=True, vmem_limit_bytes=67043328),
        cost_estimate=pl.CostEstimate(flops=12 * macs, bytes_accessed=8 << 20, transcendentals=macs // hdim),
        name="attention",
    )(cit, slot_of, vis, q4, g4, kv, own)


def body(queries, traj_kv, grad_out, doc_kv, citations, doc_slot, visible_from):
    tlen, heads_local, hdim = queries.shape
    kv_local = traj_kv.shape[1]
    group = heads_local // kv_local
    split = (tlen, kv_local, group, hdim)
    attended, d_queries, d_traj, d_doc = attention(
        citations.T, doc_slot, visible_from, queries.reshape(split), grad_out.reshape(split), traj_kv, doc_kv)
    return (attended.reshape(queries.shape), d_queries.reshape(queries.shape), d_traj,
            d_doc.reshape(doc_kv.shape))


def solution(mesh):
    in_specs = (
        P("dp", "head", None),
        P("dp", "head", None, None),
        P("dp", "head", None),
        P("dp", "head", None, None, None),
        P(),
        P(),
        P("dp", None),
    )
    out_specs = (
        P("dp", "head", None),
        P("dp", "head", None),
        P("dp", "head", None, None),
        P("dp", "head", None, None, None),
    )
    return jax.shard_map(body, mesh=mesh, in_specs=in_specs, out_specs=out_specs, check_vma=False)
```

```python
import functools
import math

import jax
import jax.numpy as jnp
from jax import lax
from jax.experimental import pallas as pl
from jax.experimental.pallas import tpu as pltpu
from jax.sharding import PartitionSpec as P

SEG = 64
BIG = 3.0e38
NT = (((1,), (1,)), ((), ()))
NN = (((1,), (0,)), ((), ()))
NX, NZ, NC, NY = 4, 4, 2, 4
FAR = (2, 1, 3)
f32 = jnp.float32
bf16 = jnp.bfloat16


def kernel(cit, slot_of, vis, q_hbm, g_hbm, kv_ref, doc_ref, o_hbm, dq_hbm, dkv_ref, dd_ref, *scratch):
    (tab, q_ref, g_ref, o_ref, dq_ref, move) = scratch[:6]
    own_ref = scratch[-1]
    (qs, gs, gn, gt, ks, vs, kt, vt, sc, pp, ds, dk, dv, inv, delta) = scratch[6:21]
    bufs = scratch[21:]
    st, rowa, rowb, senda, sendb, recva, recvb, backa, backb, suma, sumb, tot, home = (
        bufs[4 * i : 4 * i + 4] for i in range(13)
    )
    sems = bufs[52:-1]
    me, y = lax.axis_index("dp"), lax.axis_index("head")
    x, z, c = me // (NZ * NC), (me // NC) % NZ, me % NC
    tlen, nkv, group, hdim = q_ref.shape
    dlen = st[0].shape[1]
    cites = cit.shape[0]
    ndoc = cites * dlen
    rows = SEG * group
    nseg = tlen // SEG
    nch = ndoc // (2 * dlen)
    scale = 1.0 / math.sqrt(hdim)
    c1 = scale * math.log2(math.e)
    part = dlen // NY
    top, low = slice(0, dlen // 2), slice(dlen // 2, dlen)
    AIDX, BIDX, OWNER, ACITE, BCITE, ARED, BRED = range(7)

    def at(dx, dz, dc, dy):
        dp = (((x + dx) % NX) * NZ + (z + dz) % NZ) * NC + (c + dc) % NC
        return (dp, (y + dy) % NY)

    def copy(stage, k, i, src, dst, to):
        return pltpu.make_async_remote_copy(
            src_ref=src, dst_ref=dst, send_sem=sems[2 * stage].at[k, i], recv_sem=sems[2 * stage + 1].at[k, i],
            device_id=at(*to), device_id_type=pl.DeviceIdType.MESH)

    def tokens_of(i):
        return pl.ds(pl.multiple_of(i * part, part), part)

    def heads_out(k):
        return [copy(0, k, i, own_ref.at[(y + dy) % NY, k], st[k].at[:, tokens_of(y), :], (0, 0, 0, dy))
                for i, dy in enumerate(FAR)]

    def lines_out(k):
        a = [copy(1, k, i, st[k].at[:, top, :], rowa[k].at[pl.ds(x * 4, 4)], (d, 0, 0, 0)) for i, d in enumerate(FAR)]
        b = [copy(1, k, 3 + i, st[k].at[:, low, :], rowb[k].at[pl.ds(z * 4, 4)], (0, d, 0, 0)) for i, d in enumerate(FAR)]
        return [r for ab in zip(a, b) for r in ab]

    def cross(stage, k, dsta, dstb):
        hops = [(d, dc) for d in FAR for dc in range(NC)] + [(0, 1)]
        res = []
        for i, (d, dc) in enumerate(hops):
            other = (c + dc) % NC
            ja = ((z + d) % NZ) * NC + other
            jb = ((x + d) % NX) * NC + other
            res.append(copy(stage, k, i, senda[k].at[pl.ds(ja * 4, 4)], dsta[k].at[pl.ds((z * NC + c) * 4, 4)], (0, d, dc, 0)))
            res.append(copy(stage, k, 7 + i, sendb[k].at[pl.ds(jb * 4, 4)], dstb[k].at[pl.ds((x * NC + c) * 4, 4)], (d, 0, dc, 0)))
        return res

    def docs_out(k):
        return cross(2, k, recva, recvb)

    def grads_out(k):
        return cross(3, k, backa, backb)

    def sums_out(k):
        a = [copy(4, k, i, rowa[k].at[pl.ds((x + d) % NX * 4, 4)], suma[k].at[pl.ds(x * 4, 4)], (d, 0, 0, 0))
             for i, d in enumerate(FAR)]
        b = [copy(4, k, 3 + i, rowb[k].at[pl.ds((z + d) % NZ * 4, 4)], sumb[k].at[pl.ds(z * 4, 4)], (0, d, 0, 0))
             for i, d in enumerate(FAR)]
        return [r for ab in zip(a, b) for r in ab]

    def heads_home(k):
        return [copy(5, k, i, tot[k].at[:, tokens_of((y + dy) % NY), :], home[k].at[y], (0, 0, 0, dy))
                for i, dy in enumerate(FAR)]

    def start(copies):
        for r in copies:
            r.start()

    def wait(copies):
        for r in copies:
            r.wait()

    def send_lines(k):
        wait(heads_out(k))
        start(lines_out(k))
        rowa[k][pl.ds(x * 4, 4)] = st[k][:, top, :]
        rowb[k][pl.ds(z * 4, 4)] = st[k][:, low, :]

    def keep(k, dsta, dstb):
        ja, jb = (z * NC + c) * 4, (x * NC + c) * 4
        dsta[k][pl.ds(ja, 4)] = senda[k][pl.ds(ja, 4)]
        dstb[k][pl.ds(jb, 4)] = sendb[k][pl.ds(jb, 4)]

    def send_docs(k):
        wait(lines_out(k))

        @pl.loop(0, 32)
        def _(j):
            senda[k][j] = rowa[k][j % 4 * 4 + jnp.maximum(tab[ARED, j], 0)]
            sendb[k][j] = rowb[k][j % 4 * 4 + jnp.maximum(tab[BRED, j], 0)]

        start(docs_out(k))
        keep(k, recva, recvb)

    def gather(k, dst, dst_t):
        wait(docs_out(k))

        @pl.loop(0, cites)
        def _(i):
            a = recva[k][tab[AIDX, i]]
            b = recvb[k][tab[BIDX, i]]
            dst[pl.ds(pl.multiple_of(i * dlen, dlen), dlen // 2), :] = a
            dst[pl.ds(pl.multiple_of(i * dlen + dlen // 2, dlen // 2), dlen // 2), :] = b
            r = pl.ds(pl.multiple_of(i * dlen, dlen), dlen)
            dst_t[:, r] = dst[r, :].T

    def send_grads(k, src, factor):
        @pl.loop(0, 32)
        def _(j):
            senda[k][j] = (src[tab[ACITE, j]][top] * factor).astype(bf16)
            sendb[k][j] = (src[tab[BCITE, j]][low] * factor).astype(bf16)

        start(grads_out(k))
        keep(k, backa, backb)

    def send_sums(k):
        wait(grads_out(k))
        for back, row, red in ((backa, rowa, ARED), (backb, rowb, BRED)):
            @pl.loop(0, 4)
            def _(o):
                acc = [jnp.zeros((dlen // 2, hdim), f32)] * 4
                for t in range(8):
                    blk = back[k][t * 4 + o].astype(f32)
                    w = tab[red, t * 4 + o]
                    for d in range(4):
                        acc[d] = acc[d] + blk * jnp.where(w == d, 1.0, 0.0)
                for d in range(4):
                    row[k][o * 4 + d] = acc[d].astype(bf16)

        start(sums_out(k))
        suma[k][pl.ds(x * 4, 4)] = rowa[k][pl.ds(x * 4, 4)]
        sumb[k][pl.ds(z * 4, 4)] = rowb[k][pl.ds(z * 4, 4)]

    def send_home(k):
        wait(sums_out(k))
        for half, s in ((top, suma), (low, sumb)):
            for d in range(4):
                tot[k][d, half] = (s[k][d].astype(f32) + s[k][4 + d].astype(f32)
                                   + s[k][8 + d].astype(f32) + s[k][12 + d].astype(f32)).astype(bf16)
        start(heads_home(k))
        home[k][y] = tot[k][:, tokens_of(y), :]

    def finish(k):
        wait(heads_home(k))
        for i in range(NY):
            dd_ref[pl.ds(i * 4 + k, 4 * part, stride=4 * NY), :] = home[k][i].reshape(4 * part, hdim).astype(f32)

    def loads():
        return [pltpu.make_async_copy(q_hbm, q_ref, move.at[0]), pltpu.make_async_copy(g_hbm, g_ref, move.at[1])]

    def store(i, g):
        src, dst = ((o_ref, o_hbm), (dq_ref, dq_hbm))[i]
        return pltpu.make_async_copy(src.at[:, g], dst.at[:, g], move.at[2 + 2 * i + g])

    def tables():
        def pair(v):
            return (v >> 2) & 7

        for i in range(cites):
            v = slot_of[cit[i, me]]
            tab[OWNER, i] = v >> 2
            tab[AIDX, i] = pair(v) * 4 + (v >> 5)
            tab[BIDX, i] = ((v >> 5) * 2 + ((v >> 2) & 1)) * 4 + ((v >> 3) & 3)

        @pl.loop(0, 8)
        def _(t):
            a = [jnp.int32(-1)] * 4
            b = [jnp.int32(-1)] * 4
            for i in range(cites):
                v = slot_of[cit[i, x * 8 + t]]
                to = jnp.where(pair(v) == z * NC + c, v >> 5, -1)
                u = slot_of[cit[i, t // 2 * 8 + z * NC + t % 2]]
                uo = jnp.where(((u >> 5) == x) & (((u >> 2) & 1) == c), (u >> 3) & 3, -1)
                for o in range(4):
                    a[o] = jnp.where(to == o, v & 3, a[o])
                    b[o] = jnp.where(uo == o, u & 3, b[o])
            for o in range(4):
                tab[ARED, t * 4 + o] = a[o]
                tab[BRED, t * 4 + o] = b[o]

        @pl.loop(0, 32)
        def _(j):
            a, b = jnp.int32(0), jnp.int32(0)
            for i in range(cites):
                v = tab[OWNER, i]
                a = jnp.where(v == j % 4 * 8 + j // 4, i, a)
                b = jnp.where(v == j // 8 * 8 + j % 4 * 2 + j // 4 % 2, i, b)
            tab[ACITE, j] = a
            tab[BCITE, j] = b

    start(loads())
    def lay_out(g):
        for i in range(NY):
            t = doc_ref[:, :, i * nkv + g].astype(f32)
            for h in range(2):
                own_ref[i, g * 2 + h] = t[:, :, h].astype(bf16)

    lay_out(0)
    barrier = pltpu.get_barrier_semaphore()
    near = [(d, 0, dc, 0) for d in range(NX) for dc in range(NC) if d or dc]
    near += [(0, d, dc, 0) for d in FAR for dc in range(NC)] + [(0, 0, 0, d) for d in FAR]
    for to in near:
        pl.semaphore_signal(barrier, inc=1, device_id=at(*to), device_id_type=pl.DeviceIdType.MESH)
    pl.semaphore_wait(barrier, len(near))

    def send_heads(k):
        start(heads_out(k))
        st[k][:, tokens_of(y), :] = own_ref[y, k]

    def prepare(g):
        qs[...] = q_ref[:, g].astype(f32).reshape(tlen * group, hdim).astype(bf16)
        gs[...] = g_ref[:, g].astype(f32).reshape(tlen * group, hdim)
        own = kv_ref[:, g].astype(f32)
        for i, (a, b) in enumerate(((ks, kt), (vs, vt))):
            t = own[:, i].astype(bf16)
            a[ndoc:, :] = t
            b[:, ndoc:] = t.T

    send_heads(0)
    send_heads(1)
    tables()
    send_lines(0)
    lay_out(1)
    send_heads(2)
    send_heads(3)
    wait(loads())
    prepare(0)
    send_docs(0)
    send_lines(1)

    @pl.loop(0, nkv)
    def _(g):
        def second_head():
            prepare(1)
            gather(2, ks, kt)

        pl.when(g == 0)(lambda: gather(0, ks, kt))
        pl.when(g == 1)(second_head)

        @pl.loop(0, nseg)
        def _(s):
            pl.when((g == 0) & (s == 1))(lambda: send_docs(1))
            pl.when((g == 0) & (s == 3))(lambda: send_lines(2))
            rs = pl.ds(pl.multiple_of(s * rows, rows), rows)
            q = qs[rs, :]
            m = jnp.full((8, rows), -BIG, f32)
            for i in range(nch + 1):
                r = slice(i * 2 * dlen, (i + 1) * 2 * dlen)
                score = lax.dot_general(ks[r, :], q, NT, preferred_element_type=f32)
                if i == nch:
                    key = lax.broadcasted_iota(jnp.int32, (tlen, rows), 0)
                    tok = s * SEG + lax.broadcasted_iota(jnp.int32, (tlen, rows), 1) // group
                    score = jnp.where(key <= tok, score, -BIG)
                    m = jnp.maximum(m, jnp.max(score.reshape(tlen // 8, 8, rows), axis=0))
                else:
                    for h in range(2):
                        t = jnp.max(score[h * dlen : (h + 1) * dlen].reshape(dlen // 8, 8, rows), axis=0)
                        m = jnp.maximum(m, jnp.where(s >= vis[0, 2 * i + h], t, -BIG))
                sc[r, :] = score
            m = jnp.max(m, axis=0, keepdims=True)
            total = jnp.zeros((8, rows), f32)
            for i in range(2 * nch + 2):
                r = slice(i * dlen, (i + 1) * dlen)
                mm = m if i >= 2 * nch else jnp.where(s >= vis[0, i], m, BIG)
                p = jnp.exp2((sc[r, :] - mm) * c1)
                total = total + jnp.sum(p.reshape(dlen // 8, 8, rows), axis=0)
                pp[r, rs] = p.astype(bf16)
            inv[s] = 1.0 / jnp.sum(total, axis=0, keepdims=True)

        def more_docs():
            gather(1, vs, vt)
            send_lines(3)

        pl.when(g == 0)(more_docs)
        pl.when(g == 1)(lambda: gather(3, vs, vt))
        pl.when(g == 1)(lambda: send_sums(1))

        @pl.loop(0, nseg)
        def _(s):
            rs = pl.ds(pl.multiple_of(s * rows, rows), rows)
            block = pl.ds(pl.multiple_of(s * SEG, SEG), SEG)
            ot = lax.dot_general(vt[...], pp[:, rs], NN, preferred_element_type=f32)
            ot = (ot * inv[s]).astype(bf16).astype(f32)
            o_ref[block, g] = ot.T.reshape(SEG, group, hdim).astype(bf16)
            gf = gs[rs, :].T
            delta[s] = jnp.sum(ot * gf, axis=0, keepdims=True) * inv[s]
            gf = gf * inv[s]
            gn[rs, :] = gf.T.astype(bf16)
            gt[:, rs] = gf.astype(bf16)

        def contract(dst, a, b):
            @pl.loop(0, (nch + 1) // 3)
            def _(i):
                r = pl.ds(pl.multiple_of(i * 6 * dlen, 6 * dlen), 6 * dlen)
                t = lax.dot_general(a[r, :], b[...], NN, preferred_element_type=f32)
                dst[pl.ds(i * 6, 6)] = t.reshape(6, dlen, hdim)

        def first_back():
            send_sums(0)

        pl.when(g == 0)(lambda: store(0, 0).start())
        pl.when(g == 1)(lambda: store(0, 1).start())
        pl.when(g == 0)(lambda: send_docs(2))
        pl.when(g == 1)(first_back)
        contract(dv, pp, gn)
        pl.when(g == 0)(lambda: send_docs(3))
        pl.when(g == 0)(lambda: send_grads(1, dv, 1.0))
        pl.when(g == 1)(lambda: send_grads(3, dv, 1.0))

        @pl.loop(0, nseg)
        def _(s):
            rs = pl.ds(pl.multiple_of(s * rows, rows), rows)
            block = pl.ds(pl.multiple_of(s * SEG, SEG), SEG)
            for i in range(nch + 1):
                r = slice(i * 2 * dlen, (i + 1) * 2 * dlen)
                dp = lax.dot_general(vs[r, :], gt[:, rs], NN, preferred_element_type=f32)
                ds[r, rs] = pp[r, rs] * (dp - delta[s]).astype(bf16)
            dqt = lax.dot_general(kt[...], ds[:, rs], NN, preferred_element_type=f32) * scale
            dq_ref[block, g] = dqt.T.reshape(SEG, group, hdim).astype(bf16)

        pl.when(g == 0)(lambda: store(1, 0).start())
        pl.when(g == 1)(lambda: store(1, 1).start())
        contract(dk, ds, qs)

        def first_grads():
            send_grads(0, dk, scale)

        pl.when(g == 0)(first_grads)
        pl.when(g == 1)(lambda: send_grads(2, dk, scale))
        for i, t in enumerate((dk[cites:] * scale, dv[cites:])):
            dkv_ref[:, g, i] = t.reshape(tlen, hdim).astype(bf16)

    send_home(1)
    send_home(0)
    send_sums(3)
    finish(1)
    send_sums(2)
    send_home(3)
    finish(0)
    wait([store(i, g) for i in range(2) for g in range(2)])
    send_home(2)
    finish(3)
    finish(2)


def attention(cit, slot_of, vis, q4, g4, kv, own):
    tlen, nkv, group, hdim = q4.shape
    docs_dev, dlen_local = own.shape[:2]
    dlen = NY * dlen_local
    cites = cit.shape[0]
    keys = cites * dlen + tlen
    nseg, rows, all_rows = tlen // SEG, SEG * group, tlen * group
    macs = all_rows * keys * hdim * nkv

    def vmem(shape, dtype=bf16):
        return pltpu.VMEM(shape, dtype)

    scratch = [pltpu.SMEM((7, 32), jnp.int32)] + [vmem(q4.shape)] * 4 + [pltpu.SemaphoreType.DMA((6,))]
    scratch += [
        vmem((all_rows, hdim)), vmem((all_rows, hdim), f32), vmem((all_rows, hdim)), vmem((hdim, all_rows)),
        vmem((keys, hdim)), vmem((keys, hdim)), vmem((hdim, keys)), vmem((hdim, keys)),
        vmem((keys, rows), f32), vmem((keys, all_rows)), vmem((keys, all_rows)),
        vmem((keys // dlen, dlen, hdim), f32), vmem((keys // dlen, dlen, hdim), f32),
        vmem((nseg, 1, rows), f32), vmem((nseg, 1, rows), f32),
    ]
    scratch += [vmem((4, dlen, hdim))] * 4
    for n in (16, 16, 32, 32, 32, 32, 32, 32, 16, 16):
        scratch += [vmem((n, dlen // 2, hdim))] * 4
    scratch += [vmem((4, dlen, hdim))] * 4
    scratch += [vmem((NY, 4, dlen // NY, hdim))] * 4
    for n in (3, 6, 14, 14, 6, 3):
        scratch += [pltpu.SemaphoreType.DMA((4, n))] * 2
    scratch += [vmem((NY, 2 * nkv, docs_dev, dlen_local, hdim))]
    whole = pl.BlockSpec(memory_space=pltpu.VMEM)
    return pl.pallas_call(
        kernel,
        out_shape=(jax.ShapeDtypeStruct(q4.shape, bf16), jax.ShapeDtypeStruct(q4.shape, bf16),
                   jax.ShapeDtypeStruct(kv.shape, bf16), jax.ShapeDtypeStruct((own.size // hdim, hdim), f32)),
        in_specs=[pl.BlockSpec(memory_space=pltpu.SMEM)] * 3 + [pl.BlockSpec(memory_space=pl.ANY)] * 2 + [whole] * 2,
        out_specs=(pl.BlockSpec(memory_space=pl.ANY),) * 2 + (whole,) * 2,
        scratch_shapes=scratch,
        compiler_params=pltpu.CompilerParams(
            collective_id=0, has_side_effects=True, vmem_limit_bytes=67043328),
        cost_estimate=pl.CostEstimate(flops=12 * macs, bytes_accessed=8 << 20, transcendentals=macs // hdim),
        name="attention",
    )(cit, slot_of, vis, q4, g4, kv, own)


def body(queries, traj_kv, grad_out, doc_kv, citations, doc_slot, visible_from):
    tlen, heads_local, hdim = queries.shape
    kv_local = traj_kv.shape[1]
    group = heads_local // kv_local
    split = (tlen, kv_local, group, hdim)
    attended, d_queries, d_traj, d_doc = attention(
        citations.T, doc_slot, visible_from, queries.reshape(split), grad_out.reshape(split), traj_kv, doc_kv)
    return (attended.reshape(queries.shape), d_queries.reshape(queries.shape), d_traj,
            d_doc.reshape(doc_kv.shape))


def solution(mesh):
    in_specs = (
        P("dp", "head", None),
        P("dp", "head", None, None),
        P("dp", "head", None),
        P("dp", "head", None, None, None),
        P(),
        P(),
        P("dp", None),
    )
    out_specs = (
        P("dp", "head", None),
        P("dp", "head", None),
        P("dp", "head", None, None),
        P("dp", "head", None, None, None),
    )
    return jax.shard_map(body, mesh=mesh, in_specs=in_specs, out_specs=out_specs, check_vma=False)
```
